32 devices in a mesh: kv: 4 (over y, x), seq: 8 (over z, core).
Axes of the slice: x: 2, y: 2, z: 4, core: 2. Of those that a mesh axis runs over, the one named last changes fastest.
Arguments:
- hidden_in: bfloat16 [4, 16384], P(None, 'seq'), may hold values from -6 to 6
- norm_gain: float32 [16384], P('seq'), may hold values from 0.1 to 1.9
- w_query: bfloat16 [16384, 16384], P('seq', 'kv'), may hold values from -0.046875 to 0.046875
- w_key: bfloat16 [16384, 1024], P('seq', 'kv'), may hold values from -0.046875 to 0.046875
- w_value: bfloat16 [16384, 1024], P('seq', 'kv'), may hold values from -0.046875 to 0.046875
- key_cache: bfloat16 [4, 8192, 1024], P(None, 'seq', 'kv'), may hold values from -400 to 400
- value_cache: bfloat16 [4, 8192, 1024], P(None, 'seq', 'kv'), may hold values from -6 to 6
- lengths: int32 [4], replicated, may hold values from 1 to 8192
- w_out: bfloat16 [16384, 16384], P('kv', 'seq'), may hold values from -2 to 2
Outputs:
- layer_out: bfloat16 [4, 16384], P(None, 'seq')
The draws below stay inside these ranges and needn't reach their ends.
Inputs may be any that keep to these rules, and one draw needn't show every extreme that they name: The new token of sequence b follows its lengths[b] cached positions.
All inputs are finite; a program needn't handle non-finite values.
Results may differ from the reference program's by a relative error of at most 0.0095.
The reference program's roundings to bfloat16 on the way (of `normed`, `query` and `attended`) count: a program that leaves them out, or rounds other values in their place, can miss the bound.
Values may be sent and summed in bfloat16 or wider, within the bound.
No kernel may reach another device: no remote copies, remote signals or barrier semaphores. Data moves between devices by JAX's collectives and lax.ppermute only.
A program may use at most 128 MiB of HBM per device.

```python
import math
import jax
import jax.numpy as jnp
from jax import lax

D = 16384
HEADS = 128
KV_HEADS = 8
HEAD_DIM = 128
BATCH = 4
CONTEXT = 8192


def draw_key_cache(key, part):
    first_key = jax.random.fold_in(jax.random.fold_in(key, 71), 0)
    values = jax.random.normal(first_key, (BATCH, CONTEXT, KV_HEADS * HEAD_DIM), jnp.float32)
    values = values * 1.5
    return jnp.clip(values, -400.0, 400.0).astype(jnp.bfloat16)


def set_ends(entries, stream_key, low, top_value):
    longest = entries.shape.index(max(entries.shape))
    spots = []
    for shift in (0, 1):
        where = [jax.random.randint(jax.random.fold_in(stream_key, axis), (), 0, length) for axis, length in enumerate(entries.shape)]
        where[longest] = (where[longest] + shift) % entries.shape[longest]
        spots.append(tuple(where))
    return entries.at[spots[0]].set(low).at[spots[1]].set(top_value)


def block_levels(own_key, shape, cuts, low, largest):
    def one(dim, blocks):
        steps = jax.random.uniform(jax.random.fold_in(jax.random.fold_in(own_key, 6), dim), (blocks,), jnp.float32, low / len(cuts), largest / len(cuts))
        return jnp.repeat(jnp.exp(steps), shape[dim] // blocks).reshape((-1,) + (1,) * (len(shape) - dim - 1))

    factor_of = one(*cuts[0])
    for cut in cuts[1:]:
        factor_of = factor_of * one(*cut)
    return factor_of


def gaussian(rng, shape, deviation, most, pieces=(), kind=jnp.bfloat16):
    result = jax.random.normal(rng, shape, jnp.float32) * deviation
    if len(pieces) > 0:
        result = block_levels(rng, shape, pieces, -0.22, 0.18) * result
    return jnp.clip(result, min=-most, max=most).astype(kind)


def setup_inputs(seed: int = 0) -> dict:
    key_list = jax.random.split(jax.random.key(seed), 10)
    hidden_in = gaussian(key_list[0], (BATCH, D), 1.0, 6.0, ((1, 8),))
    norm_gain = jnp.clip(1.0 + 0.18 * jax.random.normal(key_list[1], (D,), jnp.float32), 0.1, 1.9)
    w_query = gaussian(key_list[2], (D, HEADS * HEAD_DIM), D ** -0.5, 0.046875, ((0, 8), (1, 4)))
    w_key = gaussian(key_list[3], (D, KV_HEADS * HEAD_DIM), D ** -0.5, 0.046875, ((0, 8), (1, 4)))
    w_value = gaussian(key_list[4], (D, KV_HEADS * HEAD_DIM), D ** -0.5, 0.046875, ((0, 8), (1, 4)))
    key_cache = draw_key_cache(jax.random.fold_in(key_list[9], 71), 0)
    value_cache = gaussian(key_list[6], (BATCH, CONTEXT, KV_HEADS * HEAD_DIM), 1.0, 6.0, ((1, 8), (2, 4)))
    lengths = set_ends(jax.random.randint(key_list[7], (BATCH,), 1, CONTEXT + 1), jax.random.fold_in(key_list[7], 1), 1, CONTEXT).astype(jnp.int32)
    w_out = gaussian(key_list[8], (HEADS * HEAD_DIM, D), 0.35, 2.0, ((0, 4), (1, 8)))
    return dict(hidden_in=hidden_in, norm_gain=norm_gain, w_query=w_query, w_key=w_key, w_value=w_value, key_cache=key_cache, value_cache=value_cache, lengths=lengths, w_out=w_out)


norm_eps = 1e-05

def head_attention(inputs, live_mask):
    query_group, key_block, value_block, key_own, value_own = inputs
    score_scale = 1.0 / math.sqrt(HEAD_DIM)
    scores = jnp.einsum('bhd,btd->bht', query_group.astype(jnp.float32), key_block.astype(jnp.float32), precision=lax.Precision.HIGHEST) * score_scale
    own_score = jnp.einsum('bhd,bd->bh', query_group.astype(jnp.float32), key_own.astype(jnp.float32), precision=lax.Precision.HIGHEST) * score_scale
    masked = jnp.where(live_mask[:, None, :], scores, jnp.float32(-1e+30))
    peak_score = jnp.maximum(lax.optimization_barrier(jnp.max(masked, axis=2)), own_score)
    weights = jnp.where(live_mask[:, None, :], jnp.exp(scores - peak_score[:, :, None]), jnp.float32(0.0))
    own_weight = jnp.exp(own_score - peak_score)
    total = lax.optimization_barrier(jnp.sum(weights, axis=2)) + own_weight
    summed = jnp.einsum('bht,btd->bhd', weights, value_block.astype(jnp.float32), precision=lax.Precision.HIGHEST)
    summed = summed + own_weight[:, :, None] * value_own.astype(jnp.float32)[:, None, :]
    return summed / total[:, :, None]

def partial_head(live_mask):

    def apply_head(inputs):
        return head_attention(inputs, live_mask)
    return apply_head

def reference(hidden_in, norm_gain, w_query, w_key, w_value, key_cache, value_cache, lengths, w_out):
    x_float = hidden_in.astype(jnp.float32)
    mean_square = lax.optimization_barrier(jnp.mean(x_float * x_float, axis=1, keepdims=True))
    row_scale = lax.rsqrt(mean_square + norm_eps)
    normed = (x_float * norm_gain.astype(jnp.float32)[None, :]).astype(jnp.bfloat16)
    query = (jnp.dot(normed, w_query, preferred_element_type=jnp.float32) * row_scale).astype(jnp.bfloat16)
    key_new = (jnp.dot(normed, w_key, preferred_element_type=jnp.float32) * row_scale).astype(jnp.bfloat16)
    value_new = (jnp.dot(normed, w_value, preferred_element_type=jnp.float32) * row_scale).astype(jnp.bfloat16)
    group_size = HEADS // KV_HEADS
    query_heads = jnp.moveaxis(query.reshape(BATCH, KV_HEADS, group_size, HEAD_DIM), 1, 0)
    key_heads = jnp.moveaxis(key_cache.reshape(BATCH, CONTEXT, KV_HEADS, HEAD_DIM), 2, 0)
    value_heads = jnp.moveaxis(value_cache.reshape(BATCH, CONTEXT, KV_HEADS, HEAD_DIM), 2, 0)
    key_owns = jnp.moveaxis(key_new.reshape(BATCH, KV_HEADS, HEAD_DIM), 1, 0)
    value_owns = jnp.moveaxis(value_new.reshape(BATCH, KV_HEADS, HEAD_DIM), 1, 0)
    positions = jnp.arange(CONTEXT, dtype=jnp.int32)
    live_mask = positions[None, :] < lengths.astype(jnp.int32)[:, None]
    results = lax.map(partial_head(live_mask), (query_heads, key_heads, value_heads, key_owns, value_owns))
    attended = jnp.moveaxis(results, 0, 1).reshape(BATCH, HEADS * HEAD_DIM).astype(jnp.bfloat16)
    projected = jnp.dot(attended, w_out, preferred_element_type=jnp.float32)
    return (x_float + projected).astype(jnp.bfloat16)
```

```python
import math

import jax
import jax.numpy as jnp
from jax import lax
from jax.experimental import pallas as pl
from jax.experimental.pallas import tpu as pltpu
from jax.sharding import PartitionSpec as P

HEAD_DIM = 128
LANES = 128
norm_eps = 1e-05
DEAD = -1e30


def swapped(array, axis, offset):
    size = lax.axis_size(axis)
    return lax.ppermute(array, axis, [(i, i ^ offset) for i in range(size)])


def stages(size, first):
    rounds, stride = [], first
    while stride < size:
        radix = 4 if size // stride % 4 == 0 else 2
        rounds.append([stride * k for k in range(1, radix)])
        stride *= radix
    return rounds


def tree_sum(terms):
    while len(terms) > 1:
        terms = [a + b for a, b in zip(terms[::2], terms[1::2])]
    return terms[0]


def vmem():
    return pl.BlockSpec(memory_space=pltpu.VMEM)


def anywhere():
    return pl.BlockSpec(memory_space=pl.ANY)


def core_index():
    return lax.rem(lax.axis_index("seq"), 2)


def project_kernel(chunks, x_ref, gain_ref, wq_hbm, wk_hbm, wv_hbm, keep_ref, send_ref, wq, wk, wv, acc, sems):
    rows = wq.shape[0] // chunks
    copies = []
    for n in range(chunks):
        part = pl.ds(n * rows, rows)
        copies.append(pltpu.make_async_copy(wq_hbm.at[part], wq.at[part], sems.at[n]))
    copies.append(pltpu.make_async_copy(wk_hbm, wk, sems.at[chunks]))
    copies.append(pltpu.make_async_copy(wv_hbm, wv, sems.at[chunks + 1]))
    for copy in copies:
        copy.start()
    x = x_ref[...].astype(jnp.float32)
    squares = jnp.sum(x * x, axis=1, keepdims=True)
    normed = (x * gain_ref[...]).astype(jnp.bfloat16)
    width = wq.shape[1]
    for n in range(chunks):
        copies[n].wait()
        part = jnp.dot(
            normed[:, n * rows : (n + 1) * rows],
            wq[n * rows : (n + 1) * rows, :],
            preferred_element_type=jnp.float32,
        )
        if n == 0:
            acc[...] = part
        elif n < chunks - 1:
            acc[...] += part
        else:
            query = acc[...] + part
    copies[chunks].wait()
    key = jnp.dot(normed, wk[...], preferred_element_type=jnp.float32)
    copies[chunks + 1].wait()
    value = jnp.dot(normed, wv[...], preferred_element_type=jnp.float32)
    first = core_index() == 0
    half = width // 2
    heads = half // LANES
    for j in range(heads):
        low = query[:, j * LANES : (j + 1) * LANES]
        high = query[:, half + j * LANES : half + (j + 1) * LANES]
        keep_ref[j] = jnp.where(first, low, high)
        send_ref[j] = jnp.where(first, high, low)
    for j, both in ((heads, key), (heads + 1, value)):
        low, high = both[:, :LANES], both[:, LANES:]
        keep_ref[j] = jnp.where(first, low, high)
        send_ref[j] = jnp.where(first, high, low)
    squares = jnp.broadcast_to(squares, (x.shape[0], LANES))
    keep_ref[heads + 2] = squares
    send_ref[heads + 2] = squares


def project(x, gain, w_query, w_key, w_value):
    depth, width = w_query.shape
    batch = x.shape[0]
    chunks = max(1, depth // 256)
    shape = jax.ShapeDtypeStruct((width // 2 // LANES + 3, batch, LANES), jnp.float32)
    size = 2 * (w_query.size + w_key.size + w_value.size)
    return pl.pallas_call(
        lambda *refs: project_kernel(chunks, *refs),
        out_shape=(shape, shape),
        in_specs=[vmem(), vmem(), anywhere(), anywhere(), anywhere()],
        out_specs=(vmem(), vmem()),
        scratch_shapes=[
            pltpu.VMEM(w_query.shape, w_query.dtype),
            pltpu.VMEM(w_key.shape, w_key.dtype),
            pltpu.VMEM(w_value.shape, w_value.dtype),
            pltpu.VMEM((batch, width), jnp.float32),
            pltpu.SemaphoreType.DMA((chunks + 2,)),
        ],
        compiler_params=pltpu.CompilerParams(vmem_limit_bytes=size + (4 << 20)),
        cost_estimate=pl.CostEstimate(flops=batch * size, bytes_accessed=size, transcendentals=0),
        name="project",
    )(x, gain.reshape(1, depth), w_query, w_key, w_value)


def attend_kernel(width, lengths_ref, own_ref, other_ref, k_hbm, v_hbm, keep_ref, send_ref, kbuf, vbuf, sems):
    batch, ctx = kbuf.shape[0], kbuf.shape[1]
    group = own_ref.shape[0] - 3
    copies = []
    for b in range(batch):
        copies.append(pltpu.make_async_copy(k_hbm.at[b], kbuf.at[b], sems.at[0, b]))
        copies.append(pltpu.make_async_copy(v_hbm.at[b], vbuf.at[b], sems.at[1, b]))
    for copy in copies:
        copy.start()
    me = lax.axis_index("seq")
    first = core_index() == 0
    holds_new = me == 0
    row_scale = lax.rsqrt(own_ref[group + 2] / width + norm_eps)
    score_scale = 1.0 / math.sqrt(HEAD_DIM)
    lane = lax.broadcasted_iota(jnp.int32, (group, LANES), 1)
    sub = lax.broadcasted_iota(jnp.int32, (group, LANES), 0)
    position = me * ctx + lax.broadcasted_iota(jnp.int32, (1, ctx), 1)
    zero = jnp.zeros((group, LANES), jnp.bfloat16)
    tops = [jnp.zeros((1, LANES), jnp.float32)] * 2
    sums = [jnp.zeros((1, LANES), jnp.float32)] * 2

    def rounded(value):
        return value.astype(jnp.bfloat16)

    for b in range(batch):
        scale = row_scale[b : b + 1, :]
        mine = rounded(own_ref[0:group, b, :] * scale)
        theirs = rounded(other_ref[0:group, b, :] * scale)
        q_low = jnp.where(first, mine, theirs)
        q_high = jnp.where(first, theirs, mine)
        q = jnp.concatenate(
            [jnp.concatenate([q_low, zero], 1), jnp.concatenate([zero, q_high], 1)], 0
        )
        new = []
        for row in (group, group + 1):
            a = rounded(own_ref[row, b : b + 1, :] * scale).astype(jnp.float32)
            o = rounded(other_ref[row, b : b + 1, :] * scale).astype(jnp.float32)
            new.append((jnp.where(first, a, o), jnp.where(first, o, a)))
        own_score = jnp.concatenate(
            [
                jnp.sum(part.astype(jnp.float32) * key, axis=1, keepdims=True)
                for part, key in zip((q_low, q_high), new[0])
            ],
            0,
        )
        own_score = jnp.where(holds_new, own_score * score_scale, DEAD)
        copies[2 * b].wait()
        scores = lax.dot_general(
            q, kbuf[b], (((1,), (1,)), ((), ())), preferred_element_type=jnp.float32
        )
        live = position < lengths_ref[b]
        scores = jnp.where(live, scores * score_scale, DEAD)
        top = jnp.maximum(jnp.max(scores, axis=1, keepdims=True), own_score)
        weights = jnp.where(live, jnp.exp(scores - top), 0.0)
        own_weight = jnp.where(holds_new, jnp.exp(own_score - top), 0.0)
        total = jnp.sum(weights, axis=1, keepdims=True) + own_weight
        high = weights.astype(jnp.bfloat16)
        low = (weights - high.astype(jnp.float32)).astype(jnp.bfloat16)
        copies[2 * b + 1].wait()
        both = jnp.dot(
            jnp.concatenate([high, low], 0), vbuf[b], preferred_element_type=jnp.float32
        )
        both = both[: 2 * group] + both[2 * group :]
        parts = []
        for g in range(2):
            rows = slice(g * group, (g + 1) * group)
            parts.append(both[rows, g * LANES : (g + 1) * LANES] + own_weight[rows] * new[1][g])
            spot = lane == sub + b * group
            tops[g] = tops[g] + jnp.sum(jnp.where(spot, top[rows], 0.0), axis=0, keepdims=True)
            sums[g] = sums[g] + jnp.sum(jnp.where(spot, total[rows], 0.0), axis=0, keepdims=True)
        keep_ref[0:group, b, :] = jnp.where(first, parts[0], parts[1])
        send_ref[0:group, b, :] = jnp.where(first, parts[1], parts[0])
    for row, pair in ((0, tops), (1, sums)):
        keep_ref[group, row : row + 1, :] = jnp.where(first, pair[0], pair[1])
        send_ref[group, row : row + 1, :] = jnp.where(first, pair[1], pair[0])
    blank = jnp.zeros((batch - 2, LANES), jnp.float32)
    keep_ref[group, 2:batch, :] = blank
    send_ref[group, 2:batch, :] = blank


def attend(own, other, key_cache, value_cache, lengths, width):
    batch = key_cache.shape[0]
    group = own.shape[0] - 3
    shape = jax.ShapeDtypeStruct((group + 1, batch, LANES), jnp.float32)
    size = 2 * (key_cache.size + value_cache.size)
    return pl.pallas_call(
        lambda *refs: attend_kernel(width, *refs),
        out_shape=(shape, shape),
        in_specs=[pl.BlockSpec(memory_space=pltpu.SMEM), vmem(), vmem(), anywhere(), anywhere()],
        out_specs=(vmem(), vmem()),
        scratch_shapes=[
            pltpu.VMEM(key_cache.shape, key_cache.dtype),
            pltpu.VMEM(value_cache.shape, value_cache.dtype),
            pltpu.SemaphoreType.DMA((2, batch)),
        ],
        compiler_params=pltpu.CompilerParams(vmem_limit_bytes=size + (8 << 20)),
        cost_estimate=pl.CostEstimate(flops=64 * size, bytes_accessed=size, transcendentals=0),
        name="attend",
    )(lengths, own, other, key_cache, value_cache)


def merge_kernel(last, count, *refs):
    parts, out_ref = refs[:count], refs[count]
    group, batch = parts[0].shape[0] - 1, parts[0].shape[1]
    lane = lax.broadcasted_iota(jnp.int32, (group, LANES), 1)
    sub = lax.broadcasted_iota(jnp.int32, (group, LANES), 0)
    tops = [part[group, 0:1, :] for part in parts]
    sums = [part[group, 1:2, :] for part in parts]
    top = tops[0]
    for other in tops[1:]:
        top = jnp.maximum(top, other)
    factors = [jnp.exp(own - top) for own in tops]
    total = tree_sum([f * s for f, s in zip(factors, sums)])
    if last:
        factors = factors + [total]
    for b in range(batch):
        spot = lane == sub + b * group
        columns = [
            jnp.sum(jnp.where(spot, f, 0.0), axis=1, keepdims=True) for f in factors
        ]
        mixed = tree_sum([part[0:group, b, :] * c for part, c in zip(parts, columns)])
        if last:
            mixed = (mixed / columns[-1]).astype(jnp.bfloat16).astype(jnp.float32)
        out_ref[0:group, b, :] = mixed
    if not last:
        out_ref[group, 0:1, :] = top
        out_ref[group, 1:2, :] = total
        out_ref[group, 2:batch, :] = jnp.zeros((batch - 2, LANES), jnp.float32)


def merge(parts, last):
    rows, batch, lanes = parts[0].shape
    shape = jax.ShapeDtypeStruct((rows - 1 if last else rows, batch, lanes), jnp.float32)
    return pl.pallas_call(
        lambda *refs: merge_kernel(last, len(parts), *refs),
        out_shape=shape,
        in_specs=[vmem()] * len(parts),
        out_specs=vmem(),
        compiler_params=pltpu.CompilerParams(vmem_limit_bytes=4 << 20),
        name="merge",
    )(*parts)


def output_kernel(chunks, own_ref, other_ref, w_hbm, out_ref, w, sems):
    rows = w.shape[0] // chunks
    copies = []
    for n in range(chunks):
        part = pl.ds(n * rows, rows)
        copies.append(pltpu.make_async_copy(w_hbm.at[part], w.at[part], sems.at[n]))
        copies[-1].start()
    first = core_index() == 0
    heads = own_ref.shape[0]
    attended = []
    for g in range(2):
        for j in range(heads):
            a, b = own_ref[j], other_ref[j]
            attended.append((jnp.where(first, a, b) if g == 0 else jnp.where(first, b, a)))
    attended = jnp.concatenate(attended, 1).astype(jnp.bfloat16)
    for n in range(chunks):
        copies[n].wait()
        part = jnp.dot(
            attended[:, n * rows : (n + 1) * rows],
            w[n * rows : (n + 1) * rows, :],
            preferred_element_type=jnp.float32,
        )
        if n == 0:
            out_ref[...] = part
        else:
            out_ref[...] += part


def output(own, other, w_out):
    depth, width = w_out.shape
    batch = own.shape[1]
    chunks = max(1, depth // 512)
    size = 2 * w_out.size
    return pl.pallas_call(
        lambda *refs: output_kernel(chunks, *refs),
        out_shape=jax.ShapeDtypeStruct((batch, width), jnp.float32),
        in_specs=[vmem(), vmem(), anywhere()],
        out_specs=vmem(),
        scratch_shapes=[
            pltpu.VMEM(w_out.shape, w_out.dtype),
            pltpu.SemaphoreType.DMA((chunks,)),
        ],
        compiler_params=pltpu.CompilerParams(vmem_limit_bytes=size + (4 << 20)),
        cost_estimate=pl.CostEstimate(flops=batch * size, bytes_accessed=size, transcendentals=0),
        name="output",
    )(own, other, w_out)


def local(hidden_in, norm_gain, w_query, w_key, w_value, key_cache, value_cache, lengths, w_out):
    seq, kv = lax.axis_size("seq"), lax.axis_size("kv")
    keep, send = project(hidden_in, norm_gain, w_query, w_key, w_value)
    own = keep + swapped(send, "seq", 1)
    for offsets in stages(seq, 2):
        own = tree_sum([own] + [swapped(own, "seq", k) for k in offsets])
    other = swapped(own, "seq", 1)
    keep, send = attend(own, other, key_cache, value_cache, lengths, hidden_in.shape[1] * seq)
    part = merge([keep, swapped(send, "seq", 1)], False)
    rounds = stages(seq, 2)
    for n, offsets in enumerate(rounds):
        part = merge([part] + [swapped(part, "seq", k) for k in offsets], n == len(rounds) - 1)
    other = swapped(part, "seq", 1)
    mixed = output(part, other, w_out)
    for offsets in stages(kv, 1):
        mixed = tree_sum([mixed] + [swapped(mixed, "kv", k) for k in offsets])
    return (hidden_in.astype(jnp.float32) + mixed).astype(jnp.bfloat16)


def solution(mesh):
    placed = (
        P(None, "seq"),
        P("seq"),
        P("seq", "kv"),
        P("seq", "kv"),
        P("seq", "kv"),
        P(None, "seq", "kv"),
        P(None, "seq", "kv"),
        P(),
        P("kv", "seq"),
    )
    return jax.shard_map(
        local, mesh=mesh, in_specs=placed, out_specs=P(None, "seq"), check_vma=False
    )
```

```python
import math

import jax
import jax.numpy as jnp
from jax import lax
from jax.experimental import pallas as pl
from jax.experimental.pallas import tpu as pltpu
from jax.sharding import PartitionSpec as P

HEAD_DIM = 128
LANES = 128
norm_eps = 1e-05
DEAD = -1e30


def swapped(array, axis, offset):
    size = lax.axis_size(axis)
    return lax.ppermute(array, axis, [(i, i ^ offset) for i in range(size)])


def stages(size, first):
    rounds, stride = [], first
    while stride < size:
        radix = 4 if size // stride % 4 == 0 else 2
        rounds.append([stride * k for k in range(1, radix)])
        stride *= radix
    return rounds


def tree_sum(terms):
    while len(terms) > 1:
        terms = [a + b for a, b in zip(terms[::2], terms[1::2])]
    return terms[0]


def vmem():
    return pl.BlockSpec(memory_space=pltpu.VMEM)


def in_hbm():
    return pl.BlockSpec(memory_space=pltpu.HBM)


def pinned(array):
    return pltpu.with_memory_space_constraint(array, pltpu.HBM)


def core_index():
    return lax.rem(lax.axis_index("seq"), 2)


def project_kernel(chunks, x_hbm, gain_hbm, wq_hbm, wk_hbm, wv_hbm, keep_ref, send_ref, x_ref, gain_ref, wq, wk, wv, acc, sems):
    rows = wq.shape[0] // chunks
    copies = []
    inputs = [
        pltpu.make_async_copy(x_hbm, x_ref, sems.at[chunks + 2]),
        pltpu.make_async_copy(gain_hbm, gain_ref, sems.at[chunks + 3]),
    ]
    for copy in inputs:
        copy.start()
    for n in range(chunks):
        part = pl.ds(n * rows, rows)
        copies.append(pltpu.make_async_copy(wq_hbm.at[part], wq.at[part], sems.at[n]))
    copies.append(pltpu.make_async_copy(wk_hbm, wk, sems.at[chunks]))
    copies.append(pltpu.make_async_copy(wv_hbm, wv, sems.at[chunks + 1]))
    for copy in copies:
        copy.start()
    for copy in inputs:
        copy.wait()
    x = x_ref[...].astype(jnp.float32)
    squares = jnp.sum(x * x, axis=1, keepdims=True)
    normed = (x * gain_ref[...]).astype(jnp.bfloat16)
    width = wq.shape[1]
    for n in range(chunks):
        copies[n].wait()
        part = jnp.dot(
            normed[:, n * rows : (n + 1) * rows],
            wq[n * rows : (n + 1) * rows, :],
            preferred_element_type=jnp.float32,
        )
        if n == 0:
            acc[...] = part
        elif n < chunks - 1:
            acc[...] += part
        else:
            query = acc[...] + part
    copies[chunks].wait()
    key = jnp.dot(normed, wk[...], preferred_element_type=jnp.float32)
    copies[chunks + 1].wait()
    value = jnp.dot(normed, wv[...], preferred_element_type=jnp.float32)
    first = core_index() == 0
    half = width // 2
    heads = half // LANES
    for j in range(heads):
        low = query[:, j * LANES : (j + 1) * LANES]
        high = query[:, half + j * LANES : half + (j + 1) * LANES]
        keep_ref[j] = jnp.where(first, low, high)
        send_ref[j] = jnp.where(first, high, low)
    for j, both in ((heads, key), (heads + 1, value)):
        low, high = both[:, :LANES], both[:, LANES:]
        keep_ref[j] = jnp.where(first, low, high)
        send_ref[j] = jnp.where(first, high, low)
    squares = jnp.broadcast_to(squares, (x.shape[0], LANES))
    keep_ref[heads + 2] = squares
    send_ref[heads + 2] = squares


def project(x, gain, w_query, w_key, w_value):
    depth, width = w_query.shape
    batch = x.shape[0]
    chunks = max(1, depth // 256)
    shape = jax.ShapeDtypeStruct((width // 2 // LANES + 3, batch, LANES), jnp.float32)
    size = 2 * (w_query.size + w_key.size + w_value.size)
    return pl.pallas_call(
        lambda *refs: project_kernel(chunks, *refs),
        out_shape=(shape, shape),
        in_specs=[in_hbm()] * 5,
        out_specs=(vmem(), vmem()),
        scratch_shapes=[
            pltpu.VMEM(x.shape, x.dtype),
            pltpu.VMEM((1, depth), gain.dtype),
            pltpu.VMEM(w_query.shape, w_query.dtype),
            pltpu.VMEM(w_key.shape, w_key.dtype),
            pltpu.VMEM(w_value.shape, w_value.dtype),
            pltpu.VMEM((batch, width), jnp.float32),
            pltpu.SemaphoreType.DMA((chunks + 4,)),
        ],
        compiler_params=pltpu.CompilerParams(vmem_limit_bytes=size + (4 << 20)),
        cost_estimate=pl.CostEstimate(flops=batch * size, bytes_accessed=size, transcendentals=0),
        name="project",
    )(*(pinned(a) for a in (x, gain.reshape(1, depth), w_query, w_key, w_value)))


def attend_kernel(width, lengths_ref, own_ref, other_ref, k_ref, v_ref, keep_ref, send_ref):
    batch, ctx = k_ref.shape[0], k_ref.shape[1]
    group = own_ref.shape[0] - 3
    me = lax.axis_index("seq")
    first = core_index() == 0
    holds_new = me == 0
    row_scale = lax.rsqrt(own_ref[group + 2] / width + norm_eps)
    score_scale = 1.0 / math.sqrt(HEAD_DIM)
    lane = lax.broadcasted_iota(jnp.int32, (group, LANES), 1)
    sub = lax.broadcasted_iota(jnp.int32, (group, LANES), 0)
    position = me * ctx + lax.broadcasted_iota(jnp.int32, (1, ctx), 1)
    zero = jnp.zeros((group, LANES), jnp.bfloat16)
    tops = [jnp.zeros((1, LANES), jnp.float32)] * 2
    sums = [jnp.zeros((1, LANES), jnp.float32)] * 2

    def rounded(value):
        return value.astype(jnp.bfloat16)

    for b in range(batch):
        scale = row_scale[b : b + 1, :]
        mine = rounded(own_ref[0:group, b, :] * scale)
        theirs = rounded(other_ref[0:group, b, :] * scale)
        q_low = jnp.where(first, mine, theirs)
        q_high = jnp.where(first, theirs, mine)
        q = jnp.concatenate(
            [jnp.concatenate([q_low, zero], 1), jnp.concatenate([zero, q_high], 1)], 0
        )
        new = []
        for row in (group, group + 1):
            a = rounded(own_ref[row, b : b + 1, :] * scale).astype(jnp.float32)
            o = rounded(other_ref[row, b : b + 1, :] * scale).astype(jnp.float32)
            new.append((jnp.where(first, a, o), jnp.where(first, o, a)))
        own_score = jnp.concatenate(
            [
                jnp.sum(part.astype(jnp.float32) * key, axis=1, keepdims=True)
                for part, key in zip((q_low, q_high), new[0])
            ],
            0,
        )
        own_score = jnp.where(holds_new, own_score * score_scale, DEAD)
        scores = lax.dot_general(
            q, k_ref[b], (((1,), (1,)), ((), ())), preferred_element_type=jnp.float32
        )
        live = position < lengths_ref[b]
        scores = jnp.where(live, scores * score_scale, DEAD)
        top = jnp.maximum(jnp.max(scores, axis=1, keepdims=True), own_score)
        weights = jnp.where(live, jnp.exp(scores - top), 0.0)
        own_weight = jnp.where(holds_new, jnp.exp(own_score - top), 0.0)
        total = jnp.sum(weights, axis=1, keepdims=True) + own_weight
        high = weights.astype(jnp.bfloat16)
        low = (weights - high.astype(jnp.float32)).astype(jnp.bfloat16)
        both = jnp.dot(
            jnp.concatenate([high, low], 0), v_ref[b], preferred_element_type=jnp.float32
        )
        both = both[: 2 * group] + both[2 * group :]
        parts = []
        for g in range(2):
            rows = slice(g * group, (g + 1) * group)
            parts.append(both[rows, g * LANES : (g + 1) * LANES] + own_weight[rows] * new[1][g])
            spot = lane == sub + b * group
            tops[g] = tops[g] + jnp.sum(jnp.where(spot, top[rows], 0.0), axis=0, keepdims=True)
            sums[g] = sums[g] + jnp.sum(jnp.where(spot, total[rows], 0.0), axis=0, keepdims=True)
        keep_ref[0:group, b, :] = jnp.where(first, parts[0], parts[1])
        send_ref[0:group, b, :] = jnp.where(first, parts[1], parts[0])
    for row, pair in ((0, tops), (1, sums)):
        keep_ref[group, row : row + 1, :] = jnp.where(first, pair[0], pair[1])
        send_ref[group, row : row + 1, :] = jnp.where(first, pair[1], pair[0])
    blank = jnp.zeros((batch - 2, LANES), jnp.float32)
    keep_ref[group, 2:batch, :] = blank
    send_ref[group, 2:batch, :] = blank


def attend(own, other, key_cache, value_cache, lengths, width):
    batch = key_cache.shape[0]
    group = own.shape[0] - 3
    shape = jax.ShapeDtypeStruct((group + 1, batch, LANES), jnp.float32)
    size = 2 * (key_cache.size + value_cache.size)
    return pl.pallas_call(
        lambda *refs: attend_kernel(width, *refs),
        out_shape=(shape, shape),
        in_specs=[pl.BlockSpec(memory_space=pltpu.SMEM), vmem(), vmem(), vmem(), vmem()],
        out_specs=(vmem(), vmem()),
        compiler_params=pltpu.CompilerParams(vmem_limit_bytes=size + (8 << 20)),
        cost_estimate=pl.CostEstimate(flops=64 * size, bytes_accessed=size, transcendentals=0),
        name="attend",
    )(lengths, own, other, key_cache, value_cache)


def merge_kernel(last, count, *refs):
    parts, out_ref = refs[:count], refs[count]
    group, batch = parts[0].shape[0] - 1, parts[0].shape[1]
    lane = lax.broadcasted_iota(jnp.int32, (group, LANES), 1)
    sub = lax.broadcasted_iota(jnp.int32, (group, LANES), 0)
    tops = [part[group, 0:1, :] for part in parts]
    sums = [part[group, 1:2, :] for part in parts]
    top = tops[0]
    for other in tops[1:]:
        top = jnp.maximum(top, other)
    factors = [jnp.exp(own - top) for own in tops]
    total = tree_sum([f * s for f, s in zip(factors, sums)])
    if last:
        factors = factors + [total]
    for b in range(batch):
        spot = lane == sub + b * group
        columns = [
            jnp.sum(jnp.where(spot, f, 0.0), axis=1, keepdims=True) for f in factors
        ]
        mixed = tree_sum([part[0:group, b, :] * c for part, c in zip(parts, columns)])
        if last:
            mixed = (mixed / columns[-1]).astype(jnp.bfloat16).astype(jnp.float32)
        out_ref[0:group, b, :] = mixed
    if not last:
        out_ref[group, 0:1, :] = top
        out_ref[group, 1:2, :] = total
        out_ref[group, 2:batch, :] = jnp.zeros((batch - 2, LANES), jnp.float32)


def merge(parts, last):
    rows, batch, lanes = parts[0].shape
    shape = jax.ShapeDtypeStruct((rows - 1 if last else rows, batch, lanes), jnp.float32)
    return pl.pallas_call(
        lambda *refs: merge_kernel(last, len(parts), *refs),
        out_shape=shape,
        in_specs=[vmem()] * len(parts),
        out_specs=vmem(),
        compiler_params=pltpu.CompilerParams(vmem_limit_bytes=4 << 20),
        name="merge",
    )(*parts)


def output_kernel(chunks, own_ref, other_ref, w_ref, out_ref):
    rows = w_ref.shape[0] // chunks
    total = None
    first = core_index() == 0
    heads = own_ref.shape[0]
    attended = []
    for g in range(2):
        for j in range(heads):
            a, b = own_ref[j], other_ref[j]
            attended.append((jnp.where(first, a, b) if g == 0 else jnp.where(first, b, a)))
    attended = jnp.concatenate(attended, 1).astype(jnp.bfloat16)
    for n in range(chunks):
        part = jnp.dot(
            attended[:, n * rows : (n + 1) * rows],
            w_ref[n * rows : (n + 1) * rows, :],
            preferred_element_type=jnp.float32,
        )
        total = part if n == 0 else total + part
    out_ref[...] = total.astype(out_ref.dtype)


def output(own, other, w_out):
    depth, width = w_out.shape
    batch = own.shape[1]
    chunks = max(1, depth // 512)
    size = 2 * w_out.size
    return pl.pallas_call(
        lambda *refs: output_kernel(chunks, *refs),
        out_shape=jax.ShapeDtypeStruct((batch, width), jnp.bfloat16),
        in_specs=[vmem(), vmem(), vmem()],
        out_specs=vmem(),
        compiler_params=pltpu.CompilerParams(vmem_limit_bytes=size + (4 << 20)),
        cost_estimate=pl.CostEstimate(flops=batch * size, bytes_accessed=size, transcendentals=0),
        name="output",
    )(own, other, w_out)


def local(hidden_in, norm_gain, w_query, w_key, w_value, key_cache, value_cache, lengths, w_out):
    seq, kv = lax.axis_size("seq"), lax.axis_size("kv")
    keep, send = project(hidden_in, norm_gain, w_query, w_key, w_value)
    own = keep + swapped(send, "seq", 1)
    for offsets in stages(seq, 2):
        own = tree_sum([own] + [swapped(own, "seq", k) for k in offsets])
    other = swapped(own, "seq", 1)
    keep, send = attend(own, other, key_cache, value_cache, lengths, hidden_in.shape[1] * seq)
    part = merge([keep, swapped(send, "seq", 1)], False)
    rounds = stages(seq, 2)
    for n, offsets in enumerate(rounds):
        part = merge([part] + [swapped(part, "seq", k) for k in offsets], n == len(rounds) - 1)
    other = swapped(part, "seq", 1)
    mixed = output(part, other, w_out)
    for offsets in stages(kv, 1):
        parts = [mixed] + [swapped(mixed, "kv", k) for k in offsets]
        mixed = tree_sum([part.astype(jnp.float32) for part in parts])
    return (hidden_in.astype(jnp.float32) + mixed).astype(jnp.bfloat16)


def solution(mesh):
    placed = (
        P(None, "seq"),
        P("seq"),
        P("seq", "kv"),
        P("seq", "kv"),
        P("seq", "kv"),
        P(None, "seq", "kv"),
        P(None, "seq", "kv"),
        P(),
        P("kv", "seq"),
    )
    return jax.shard_map(
        local, mesh=mesh, in_specs=placed, out_specs=P(None, "seq"), check_vma=False
    )
```

```python
import math

import jax
import jax.numpy as jnp
from jax import lax
from jax.experimental import pallas as pl
from jax.experimental.pallas import tpu as pltpu
from jax.sharding import PartitionSpec as P

HEAD_DIM = 128
LANES = 128
norm_eps = 1e-05
DEAD = -1e30


def swapped(array, axis, offset):
    size = lax.axis_size(axis)
    return lax.ppermute(array, axis, [(i, i ^ offset) for i in range(size)])


def stages(size, first):
    rounds, stride = [], first
    while stride < size:
        radix = 4 if size // stride % 4 == 0 else 2
        rounds.append([stride * k for k in range(1, radix)])
        stride *= radix
    return rounds


def tree_sum(terms):
    while len(terms) > 1:
        terms = [a + b for a, b in zip(terms[::2], terms[1::2])]
    return terms[0]


def vmem():
    return pl.BlockSpec(memory_space=pltpu.VMEM)


def in_hbm():
    return pl.BlockSpec(memory_space=pltpu.HBM)


def pinned(array):
    return pltpu.with_memory_space_constraint(array, pltpu.HBM)


def core_index():
    return lax.rem(lax.axis_index("seq"), 2)


def project_kernel(chunks, x_hbm, gain_hbm, wq_hbm, wk_hbm, wv_hbm, keep_ref, send_ref, x_ref, gain_ref, wq, wk, wv, acc, sems):
    rows = wq.shape[0] // chunks
    copies = []
    inputs = [
        pltpu.make_async_copy(x_hbm, x_ref, sems.at[chunks + 2]),
        pltpu.make_async_copy(gain_hbm, gain_ref, sems.at[chunks + 3]),
    ]
    for copy in inputs:
        copy.start()
    for n in range(chunks):
        part = pl.ds(n * rows, rows)
        copies.append(pltpu.make_async_copy(wq_hbm.at[part], wq.at[part], sems.at[n]))
    copies.append(pltpu.make_async_copy(wk_hbm, wk, sems.at[chunks]))
    copies.append(pltpu.make_async_copy(wv_hbm, wv, sems.at[chunks + 1]))
    for copy in copies:
        copy.start()
    for copy in inputs:
        copy.wait()
    x = x_ref[...].astype(jnp.float32)
    squares = jnp.sum(x * x, axis=1, keepdims=True)
    normed = (x * gain_ref[...]).astype(jnp.bfloat16)
    width = wq.shape[1]
    for n in range(chunks):
        copies[n].wait()
        part = jnp.dot(
            normed[:, n * rows : (n + 1) * rows],
            wq[n * rows : (n + 1) * rows, :],
            preferred_element_type=jnp.float32,
        )
        if n == 0:
            acc[...] = part
        elif n < chunks - 1:
            acc[...] += part
        else:
            query = acc[...] + part
    copies[chunks].wait()
    key = jnp.dot(normed, wk[...], preferred_element_type=jnp.float32)
    copies[chunks + 1].wait()
    value = jnp.dot(normed, wv[...], preferred_element_type=jnp.float32)
    first = core_index() == 0
    half = width // 2
    heads = half // LANES
    for j in range(heads):
        low = query[:, j * LANES : (j + 1) * LANES]
        high = query[:, half + j * LANES : half + (j + 1) * LANES]
        keep_ref[j] = jnp.where(first, low, high)
        send_ref[j] = jnp.where(first, high, low)
    for j, both in ((heads, key), (heads + 1, value)):
        low, high = both[:, :LANES], both[:, LANES:]
        keep_ref[j] = jnp.where(first, low, high)
        send_ref[j] = jnp.where(first, high, low)
    squares = jnp.broadcast_to(squares, (x.shape[0], LANES))
    keep_ref[heads + 2] = squares
    send_ref[heads + 2] = squares


def project(x, gain, w_query, w_key, w_value):
    depth, width = w_query.shape
    batch = x.shape[0]
    chunks = max(1, depth // 256)
    shape = jax.ShapeDtypeStruct((width // 2 // LANES + 3, batch, LANES), jnp.float32)
    size = 2 * (w_query.size + w_key.size + w_value.size)
    return pl.pallas_call(
        lambda *refs: project_kernel(chunks, *refs),
        out_shape=(shape, shape),
        in_specs=[in_hbm()] * 5,
        out_specs=(vmem(), vmem()),
        scratch_shapes=[
            pltpu.VMEM(x.shape, x.dtype),
            pltpu.VMEM((1, depth), gain.dtype),
            pltpu.VMEM(w_query.shape, w_query.dtype),
            pltpu.VMEM(w_key.shape, w_key.dtype),
            pltpu.VMEM(w_value.shape, w_value.dtype),
            pltpu.VMEM((batch, width), jnp.float32),
            pltpu.SemaphoreType.DMA((chunks + 4,)),
        ],
        compiler_params=pltpu.CompilerParams(vmem_limit_bytes=size + (4 << 20)),
        cost_estimate=pl.CostEstimate(flops=batch * size, bytes_accessed=size, transcendentals=0),
        name="project",
    )(*(pinned(a) for a in (x, gain.reshape(1, depth), w_query, w_key, w_value)))


def attend_kernel(own, width, lengths_ref, q_ref, k_ref, v_ref, out_ref):
    batch, ctx = k_ref.shape[0], k_ref.shape[1]
    group = q_ref.shape[0] - 3
    me = lax.axis_index("seq")
    head = core_index() if own else 1 - core_index()
    columns = pl.ds(pl.multiple_of(head * LANES, LANES), LANES)
    holds_new = me == 0
    row_scale = lax.rsqrt(q_ref[group + 2] / width + norm_eps)
    score_scale = 1.0 / math.sqrt(HEAD_DIM)
    lane = lax.broadcasted_iota(jnp.int32, (group, LANES), 1)
    sub = lax.broadcasted_iota(jnp.int32, (group, LANES), 0)
    position = me * ctx + lax.broadcasted_iota(jnp.int32, (1, ctx), 1)
    live = [position < lengths_ref[b] for b in range(batch)]
    query, scores, own_score, new_value = [], [], [], []
    for b in range(batch):
        scale = row_scale[b : b + 1, :]
        query.append((q_ref[0:group, b, :] * scale).astype(jnp.bfloat16))
        new_key, value = (
            (q_ref[row, b : b + 1, :] * scale).astype(jnp.bfloat16).astype(jnp.float32)
            for row in (group, group + 1)
        )
        new_value.append(value)
        score = jnp.sum(query[b].astype(jnp.float32) * new_key, axis=1, keepdims=True)
        own_score.append(jnp.where(holds_new, score * score_scale, DEAD))
    for b in range(batch):
        score = lax.dot_general(
            query[b],
            k_ref[b, :, columns],
            (((1,), (1,)), ((), ())),
            preferred_element_type=jnp.float32,
        )
        scores.append(jnp.where(live[b], score * score_scale, DEAD))
    top = [
        jnp.maximum(jnp.max(scores[b], axis=1, keepdims=True), own_score[b]) for b in range(batch)
    ]
    weights = [jnp.where(live[b], jnp.exp(scores[b] - top[b]), 0.0) for b in range(batch)]
    own_weight = [jnp.where(holds_new, jnp.exp(own_score[b] - top[b]), 0.0) for b in range(batch)]
    total = [jnp.sum(weights[b], axis=1, keepdims=True) + own_weight[b] for b in range(batch)]
    tops = jnp.zeros((1, LANES), jnp.float32)
    sums = jnp.zeros((1, LANES), jnp.float32)
    for b in range(batch):
        high = weights[b].astype(jnp.bfloat16)
        low = (weights[b] - high.astype(jnp.float32)).astype(jnp.bfloat16)
        both = jnp.dot(
            jnp.concatenate([high, low], 0),
            v_ref[b, :, columns],
            preferred_element_type=jnp.float32,
        )
        out_ref[0:group, b, :] = both[:group] + both[group:] + own_weight[b] * new_value[b]
        spot = lane == sub + b * group
        tops = tops + jnp.sum(jnp.where(spot, top[b], 0.0), axis=0, keepdims=True)
        sums = sums + jnp.sum(jnp.where(spot, total[b], 0.0), axis=0, keepdims=True)
    blank = jnp.zeros((batch - 1, LANES), jnp.float32)
    out_ref[group] = jnp.concatenate([tops, blank], 0)
    out_ref[group + 1] = jnp.concatenate([sums, blank], 0)


def attend(own, summed, key_cache, value_cache, lengths, width):
    batch = key_cache.shape[0]
    group = summed.shape[0] - 3
    size = key_cache.size + value_cache.size
    return pl.pallas_call(
        lambda *refs: attend_kernel(own, width, *refs),
        out_shape=jax.ShapeDtypeStruct((group + 2, batch, LANES), jnp.float32),
        in_specs=[pl.BlockSpec(memory_space=pltpu.SMEM), vmem(), vmem(), vmem()],
        out_specs=vmem(),
        compiler_params=pltpu.CompilerParams(vmem_limit_bytes=2 * size + (8 << 20)),
        cost_estimate=pl.CostEstimate(flops=64 * size, bytes_accessed=size, transcendentals=0),
        name="attend",
    )(lengths, summed, key_cache, value_cache)


def three_rows(row, count):
    rows, rest = [], row
    for _ in range(3):
        rows.append(rest.astype(jnp.bfloat16).astype(jnp.float32))
        rest = rest - rows[-1]
    rows.append(jnp.zeros((count - 3, row.shape[1]), jnp.float32))
    return jnp.concatenate(rows, 0)


def merge_kernel(last, count, *refs):
    parts, out_ref = list(refs[:count]), refs[count]
    wide = refs[-1]
    group, batch = parts[0].shape[0] - 2, parts[0].shape[1]
    for j, part in enumerate(parts):
        if part.dtype != jnp.float32:
            wide[j] = part[...].astype(jnp.float32)
            parts[j] = wide.at[j]
    lane = lax.broadcasted_iota(jnp.int32, (group, LANES), 1)
    sub = lax.broadcasted_iota(jnp.int32, (group, LANES), 0)

    def row_of(part, tile):
        value = part[tile]
        return (value[0:1] + value[1:2]) + value[2:3]

    tops = [row_of(part, group) for part in parts]
    sums = [row_of(part, group + 1) for part in parts]
    top = tops[0]
    for other in tops[1:]:
        top = jnp.maximum(top, other)
    factors = [jnp.exp(own - top) for own in tops]
    total = tree_sum([f * s for f, s in zip(factors, sums)])
    if last:
        factors = factors + [total]
    for b in range(batch):
        spot = lane == sub + b * group
        columns = [
            jnp.sum(jnp.where(spot, f, 0.0), axis=1, keepdims=True) for f in factors
        ]
        mixed = tree_sum([part[0:group, b, :] * c for part, c in zip(parts, columns)])
        if last:
            mixed = (mixed / columns[-1]).astype(jnp.bfloat16).astype(jnp.float32)
        out_ref[0:group, b, :] = mixed
    if not last:
        send_ref = refs[count + 1]
        blank = jnp.zeros((batch - 1, LANES), jnp.float32)
        for tile, row in ((group, top), (group + 1, total)):
            out_ref[tile] = jnp.concatenate([row, blank], 0)
            send_ref[tile] = three_rows(row, batch).astype(jnp.bfloat16)
        send_ref[0:group] = out_ref[0:group].astype(jnp.bfloat16)


def merge(parts, last):
    rows, batch, lanes = parts[0].shape
    if last:
        shape = jax.ShapeDtypeStruct((rows - 2, batch, lanes), jnp.float32)
    else:
        shape = tuple(
            jax.ShapeDtypeStruct((rows, batch, lanes), kind) for kind in (jnp.float32, jnp.bfloat16)
        )
    return pl.pallas_call(
        lambda *refs: merge_kernel(last, len(parts), *refs),
        out_shape=shape,
        in_specs=[vmem()] * len(parts),
        out_specs=vmem() if last else (vmem(), vmem()),
        scratch_shapes=[pltpu.VMEM((len(parts), rows, batch, lanes), jnp.float32)],
        compiler_params=pltpu.CompilerParams(vmem_limit_bytes=4 << 20),
        name="merge",
    )(*parts)


def output_kernel(own, steps, attended_ref, w_ref, *refs):
    out_ref = refs[-1]
    heads = attended_ref.shape[0]
    half = w_ref.shape[0] // 2
    head = 1 - core_index() if own else core_index()
    rows = half // steps
    attended = jnp.concatenate([attended_ref[j] for j in range(heads)], 1).astype(jnp.bfloat16)
    total = None if own else refs[0][...]
    for n in range(steps):
        at = pl.ds(pl.multiple_of(head * half + n * rows, rows), rows)
        part = jnp.dot(
            attended[:, n * rows : (n + 1) * rows], w_ref[at, :], preferred_element_type=jnp.float32
        )
        total = part if total is None else total + part
    out_ref[...] = total


def output(own, attended, w_out, so_far=()):
    depth, width = w_out.shape
    batch = attended.shape[1]
    size = w_out.size
    return pl.pallas_call(
        lambda *refs: output_kernel(own, max(1, depth // 1024), *refs),
        out_shape=jax.ShapeDtypeStruct((batch, width), jnp.float32),
        in_specs=[vmem()] * (2 + len(so_far)),
        out_specs=vmem(),
        compiler_params=pltpu.CompilerParams(vmem_limit_bytes=2 * size + (4 << 20)),
        cost_estimate=pl.CostEstimate(flops=batch * size, bytes_accessed=size, transcendentals=0),
        name="output",
    )(attended, w_out, *so_far)


def local(hidden_in, norm_gain, w_query, w_key, w_value, key_cache, value_cache, lengths, w_out):
    seq, kv = lax.axis_size("seq"), lax.axis_size("kv")
    keep, send = project(hidden_in, norm_gain, w_query, w_key, w_value)
    own = keep + swapped(send, "seq", 1)
    for offsets in stages(seq, 2):
        own = tree_sum([own] + [swapped(own, "seq", k) for k in offsets])
    other = swapped(own, "seq", 1)
    width = hidden_in.shape[1] * seq
    send = attend(True, own, key_cache, value_cache, lengths, width)
    keep = attend(False, other, key_cache, value_cache, lengths, width)
    part, narrow = merge([keep, swapped(send, "seq", 1)], False)
    rounds = stages(seq, 2)
    for n, offsets in enumerate(rounds):
        last = n == len(rounds) - 1
        merged = merge([part] + [swapped(narrow, "seq", k) for k in offsets], last)
        if not last:
            part, narrow = merged
    other = swapped(merged, "seq", 1)
    mixed = output(True, merged, w_out)
    mixed = output(False, other, w_out, (mixed,))
    for offsets in stages(kv, 1):
        mixed = tree_sum([mixed] + [swapped(mixed, "kv", k) for k in offsets])
    return (hidden_in.astype(jnp.float32) + mixed).astype(jnp.bfloat16)


def solution(mesh):
    placed = (
        P(None, "seq"),
        P("seq"),
        P("seq", "kv"),
        P("seq", "kv"),
        P("seq", "kv"),
        P(None, "seq", "kv"),
        P(None, "seq", "kv"),
        P(),
        P("kv", "seq"),
    )
    return jax.shard_map(
        local, mesh=mesh, in_specs=placed, out_specs=P(None, "seq"), check_vma=False
    )
```

```python
import math

import jax
import jax.numpy as jnp
from jax import lax
from jax.experimental import pallas as pl
from jax.experimental.pallas import tpu as pltpu
from jax.sharding import PartitionSpec as P

HEAD_DIM = 128
LANES = 128
norm_eps = 1e-05
DEAD = -1e30
HINT = 10**10


def swapped(array, axis, offset):
    size = lax.axis_size(axis)
    return lax.ppermute(array, axis, [(i, i ^ offset) for i in range(size)])


def stages(size, first):
    rounds, stride = [], first
    while stride < size:
        radix = 4 if size // stride % 4 == 0 else 2
        rounds.append([stride * k for k in range(1, radix)])
        stride *= radix
    return rounds


def tree_sum(terms):
    while len(terms) > 1:
        terms = [a + b for a, b in zip(terms[::2], terms[1::2])]
    return terms[0]


def vmem():
    return pl.BlockSpec(memory_space=pltpu.VMEM)


def in_hbm():
    return pl.BlockSpec(memory_space=pltpu.HBM)


def pinned(array):
    return pltpu.with_memory_space_constraint(array, pltpu.HBM)


def core_index():
    return lax.rem(lax.axis_index("seq"), 2)


def project_kernel(cuts, x_hbm, gain_hbm, wq_hbm, wk_hbm, wv_hbm, keep_ref, send_ref, x_ref, gain_ref, wq, wk, wv, acc, sems):
    pairs = [(x_hbm, x_ref), (gain_hbm, gain_ref), (wk_hbm, wk), (wv_hbm, wv)]
    for low, high in zip(cuts, cuts[1:]):
        part = pl.ds(low, high - low)
        pairs.append((wq_hbm.at[part], wq.at[part]))
    copies = [pltpu.make_async_copy(a, b, sems.at[n]) for n, (a, b) in enumerate(pairs)]
    for copy in copies:
        copy.start()
    copies[0].wait()
    copies[1].wait()
    x = x_ref[...].astype(jnp.float32)
    squares = jnp.sum(x * x, axis=1, keepdims=True)
    normed = (x * gain_ref[...]).astype(jnp.bfloat16)
    copies[2].wait()
    key = jnp.dot(normed, wk[...], preferred_element_type=jnp.float32)
    copies[3].wait()
    value = jnp.dot(normed, wv[...], preferred_element_type=jnp.float32)
    first = core_index() == 0
    half = wq.shape[1] // 2
    heads = half // LANES
    for j, both in ((heads, key), (heads + 1, value)):
        low, high = both[:, :LANES], both[:, LANES:]
        keep_ref[j] = jnp.where(first, low, high)
        send_ref[j] = jnp.where(first, high, low)
    squares = jnp.broadcast_to(squares, (x.shape[0], LANES))
    keep_ref[heads + 2] = squares
    send_ref[heads + 2] = squares
    last = len(cuts) - 2
    for n, (low, high) in enumerate(zip(cuts, cuts[1:])):
        copies[4 + n].wait()
        part = jnp.dot(
            normed[:, low:high], wq[low:high, :], preferred_element_type=jnp.float32
        )
        if n == 0:
            acc[...] = part
        elif n < last:
            acc[...] += part
        else:
            query = acc[...] + part
    for j in range(heads):
        low = query[:, j * LANES : (j + 1) * LANES]
        high = query[:, half + j * LANES : half + (j + 1) * LANES]
        keep_ref[j] = jnp.where(first, low, high)
        send_ref[j] = jnp.where(first, high, low)


def project(x, gain, w_query, w_key, w_value):
    depth, width = w_query.shape
    batch = x.shape[0]
    step = min(depth // 2, 256)
    cuts = tuple(range(0, depth - step + 1, step)) + (depth - step // 2, depth)
    shape = jax.ShapeDtypeStruct((width // 2 // LANES + 3, batch, LANES), jnp.float32)
    size = 2 * (w_query.size + w_key.size + w_value.size)
    return pl.pallas_call(
        lambda *refs: project_kernel(cuts, *refs),
        out_shape=(shape, shape),
        in_specs=[in_hbm()] * 5,
        out_specs=(vmem(), vmem()),
        scratch_shapes=[
            pltpu.VMEM(x.shape, x.dtype),
            pltpu.VMEM((1, depth), gain.dtype),
            pltpu.VMEM(w_query.shape, w_query.dtype),
            pltpu.VMEM(w_key.shape, w_key.dtype),
            pltpu.VMEM(w_value.shape, w_value.dtype),
            pltpu.VMEM((batch, width), jnp.float32),
            pltpu.SemaphoreType.DMA((len(cuts) + 3,)),
        ],
        compiler_params=pltpu.CompilerParams(vmem_limit_bytes=size + (4 << 20)),
        cost_estimate=pl.CostEstimate(flops=batch * size, bytes_accessed=size, transcendentals=0),
        name="project",
    )(*(pinned(a) for a in (x, gain.reshape(1, depth), w_query, w_key, w_value)))


def attend_kernel(straight, width, lengths_ref, q_ref, k_ref, v_ref, out_ref):
    batch, ctx = k_ref.shape[0], k_ref.shape[1]
    group = q_ref.shape[0] - 3
    me = lax.axis_index("seq")
    head = core_index() if straight else 1 - core_index()
    columns = pl.ds(pl.multiple_of(head * LANES, LANES), LANES)
    holds_new = me == 0
    row_scale = lax.rsqrt(q_ref[group + 2] / width + norm_eps)
    score_scale = 1.0 / math.sqrt(HEAD_DIM)
    lane = lax.broadcasted_iota(jnp.int32, (group, LANES), 1)
    sub = lax.broadcasted_iota(jnp.int32, (group, LANES), 0)
    position = me * ctx + lax.broadcasted_iota(jnp.int32, (1, ctx), 1)
    live = [position < lengths_ref[b] for b in range(batch)]
    query, scores, own_score, new_value = [], [], [], []
    for b in range(batch):
        scale = row_scale[b : b + 1, :]
        query.append((q_ref[0:group, b, :] * scale).astype(jnp.bfloat16))
        new_key, value = (
            (q_ref[row, b : b + 1, :] * scale).astype(jnp.bfloat16).astype(jnp.float32)
            for row in (group, group + 1)
        )
        new_value.append(value)
        score = jnp.sum(query[b].astype(jnp.float32) * new_key, axis=1, keepdims=True)
        own_score.append(jnp.where(holds_new, score * score_scale, DEAD))
    for b in range(batch):
        score = lax.dot_general(
            query[b],
            k_ref[b, :, columns],
            (((1,), (1,)), ((), ())),
            preferred_element_type=jnp.float32,
        )
        scores.append(jnp.where(live[b], score * score_scale, DEAD))
    top = [
        jnp.maximum(jnp.max(scores[b], axis=1, keepdims=True), own_score[b]) for b in range(batch)
    ]
    weights = [jnp.where(live[b], jnp.exp(scores[b] - top[b]), 0.0) for b in range(batch)]
    own_weight = [jnp.where(holds_new, jnp.exp(own_score[b] - top[b]), 0.0) for b in range(batch)]
    total = [jnp.sum(weights[b], axis=1, keepdims=True) + own_weight[b] for b in range(batch)]
    tops = jnp.zeros((1, LANES), jnp.float32)
    sums = jnp.zeros((1, LANES), jnp.float32)
    for b in range(batch):
        high = weights[b].astype(jnp.bfloat16)
        low = (weights[b] - high.astype(jnp.float32)).astype(jnp.bfloat16)
        both = jnp.dot(
            jnp.concatenate([high, low], 0),
            v_ref[b, :, columns],
            preferred_element_type=jnp.float32,
        )
        out_ref[0:group, b, :] = both[:group] + both[group:] + own_weight[b] * new_value[b]
        spot = lane == sub + b * group
        tops = tops + jnp.sum(jnp.where(spot, top[b], 0.0), axis=0, keepdims=True)
        sums = sums + jnp.sum(jnp.where(spot, total[b], 0.0), axis=0, keepdims=True)
    blank = jnp.zeros((batch - 1, LANES), jnp.float32)
    out_ref[group] = jnp.concatenate([tops, blank], 0)
    out_ref[group + 1] = jnp.concatenate([sums, blank], 0)


def attend(straight, summed, key_cache, value_cache, lengths, width):
    batch = key_cache.shape[0]
    group = summed.shape[0] - 3
    size = key_cache.size + value_cache.size
    return pl.pallas_call(
        lambda *refs: attend_kernel(straight, width, *refs),
        out_shape=jax.ShapeDtypeStruct((group + 2, batch, LANES), jnp.float32),
        in_specs=[pl.BlockSpec(memory_space=pltpu.SMEM), vmem(), vmem(), vmem()],
        out_specs=vmem(),
        compiler_params=pltpu.CompilerParams(vmem_limit_bytes=2 * size + (8 << 20)),
        cost_estimate=pl.CostEstimate(flops=HINT * 10, bytes_accessed=size, transcendentals=0),
        name="attend",
    )(lengths, summed, key_cache, value_cache)


def three_rows(row, count):
    rows, rest = [], row
    for _ in range(3):
        rows.append(rest.astype(jnp.bfloat16).astype(jnp.float32))
        rest = rest - rows[-1]
    rows.append(jnp.zeros((count - 3, row.shape[1]), jnp.float32))
    return jnp.concatenate(rows, 0)


def merge_kernel(last, count, *refs):
    parts, out_ref, wide = list(refs[:count]), refs[count], refs[-1]
    result = out_ref if last else wide.at[count]
    group, batch = parts[0].shape[0] - 2, parts[0].shape[1]
    for j, part in enumerate(parts):
        if part.dtype != jnp.float32:
            wide[j] = part[...].astype(jnp.float32)
            parts[j] = wide.at[j]
    lane = lax.broadcasted_iota(jnp.int32, (group, LANES), 1)
    sub = lax.broadcasted_iota(jnp.int32, (group, LANES), 0)

    def row_of(part, tile):
        value = part[tile]
        return (value[0:1] + value[1:2]) + value[2:3]

    tops = [row_of(part, group) for part in parts]
    sums = [row_of(part, group + 1) for part in parts]
    top = tops[0]
    for other in tops[1:]:
        top = jnp.maximum(top, other)
    factors = [jnp.exp(own - top) for own in tops]
    total = tree_sum([f * s for f, s in zip(factors, sums)])
    if last:
        factors = factors + [total]
    for b in range(batch):
        spot = lane == sub + b * group
        columns = [
            jnp.sum(jnp.where(spot, f, 0.0), axis=1, keepdims=True) for f in factors
        ]
        mixed = tree_sum([part[0:group, b, :] * c for part, c in zip(parts, columns)])
        if last:
            mixed = (mixed / columns[-1]).astype(jnp.bfloat16).astype(jnp.float32)
        result[0:group, b, :] = mixed
    if not last:
        for tile, row in ((group, top), (group + 1, total)):
            out_ref[tile] = three_rows(row, batch).astype(jnp.bfloat16)
        out_ref[0:group] = result[0:group].astype(jnp.bfloat16)


def merge(parts, last):
    rows, batch, lanes = parts[0].shape
    if last:
        shape = jax.ShapeDtypeStruct((rows - 2, batch, lanes), jnp.float32)
    else:
        shape = jax.ShapeDtypeStruct((rows, batch, lanes), jnp.bfloat16)
    return pl.pallas_call(
        lambda *refs: merge_kernel(last, len(parts), *refs),
        out_shape=shape,
        in_specs=[vmem()] * len(parts),
        out_specs=vmem(),
        scratch_shapes=[pltpu.VMEM((len(parts) + 1, rows, batch, lanes), jnp.float32)],
        compiler_params=pltpu.CompilerParams(vmem_limit_bytes=4 << 20),
        name="merge",
    )(*parts)


def output_kernel(straight, steps, attended_ref, w_ref, *refs):
    out_ref = refs[-1]
    heads = attended_ref.shape[0]
    half = w_ref.shape[0] // 2
    head = core_index() if straight else 1 - core_index()
    rows = half // steps
    attended = jnp.concatenate([attended_ref[j] for j in range(heads)], 1).astype(jnp.bfloat16)
    total = refs[0][...] if len(refs) > 1 else None
    for n in range(steps):
        at = pl.ds(pl.multiple_of(head * half + n * rows, rows), rows)
        part = jnp.dot(
            attended[:, n * rows : (n + 1) * rows], w_ref[at, :], preferred_element_type=jnp.float32
        )
        total = part if total is None else total + part
    out_ref[...] = total


def output(straight, attended, w_out, so_far=()):
    depth, width = w_out.shape
    batch = attended.shape[1]
    size = w_out.size
    return pl.pallas_call(
        lambda *refs: output_kernel(straight, max(1, depth // 1024), *refs),
        out_shape=jax.ShapeDtypeStruct((batch, width), jnp.float32),
        in_specs=[vmem()] * (2 + len(so_far)),
        out_specs=vmem(),
        compiler_params=pltpu.CompilerParams(vmem_limit_bytes=2 * size + (4 << 20)),
        cost_estimate=pl.CostEstimate(flops=batch * size, bytes_accessed=size, transcendentals=0),
        name="output",
    )(attended, w_out, *so_far)


def add_kernel(*refs):
    refs[-1][...] = tree_sum([ref[...] for ref in refs[:-1]])


def added(parts):
    return pl.pallas_call(
        add_kernel,
        out_shape=jax.ShapeDtypeStruct(parts[0].shape, parts[0].dtype),
        in_specs=[vmem()] * len(parts),
        out_specs=vmem(),
        compiler_params=pltpu.CompilerParams(vmem_limit_bytes=4 << 20),
        cost_estimate=pl.CostEstimate(flops=HINT, bytes_accessed=1024, transcendentals=0),
        name="added",
    )(*parts)


def gathered(array, offsets):
    return [swapped(array, "seq", k ^ 1) for k in [0] + offsets]


def local(hidden_in, norm_gain, w_query, w_key, w_value, key_cache, value_cache, lengths, w_out):
    seq, kv = lax.axis_size("seq"), lax.axis_size("kv")
    rounds = stages(seq, 2)
    keep, send = project(hidden_in, norm_gain, w_query, w_key, w_value)
    straight = True
    summed = added([keep, swapped(send, "seq", 1)])
    for offsets in rounds:
        summed = added(gathered(summed, offsets))
        straight = not straight
    other = swapped(summed, "seq", 1)
    width = hidden_in.shape[1] * seq
    send = attend(straight, summed, key_cache, value_cache, lengths, width)
    straight = not straight
    keep = attend(straight, other, key_cache, value_cache, lengths, width)
    merged = merge([keep, swapped(send, "seq", 1)], False)
    for n, offsets in enumerate(rounds):
        merged = merge(gathered(merged, offsets), n == len(rounds) - 1)
        straight = not straight
    other = swapped(merged, "seq", 1)
    mixed = output(straight, merged, w_out)
    mixed = output(not straight, other, w_out, (mixed,))
    for offsets in stages(kv, 1):
        mixed = tree_sum([mixed] + [swapped(mixed, "kv", k) for k in offsets])
    return (hidden_in.astype(jnp.float32) + mixed).astype(jnp.bfloat16)


def solution(mesh):
    placed = (
        P(None, "seq"),
        P("seq"),
        P("seq", "kv"),
        P("seq", "kv"),
        P("seq", "kv"),
        P(None, "seq", "kv"),
        P(None, "seq", "kv"),
        P(),
        P("kv", "seq"),
    )
    return jax.shard_map(
        local, mesh=mesh, in_specs=placed, out_specs=P(None, "seq"), check_vma=False
    )
```

```python
import math

import jax
import jax.numpy as jnp
from jax import lax
from jax.experimental import pallas as pl
from jax.experimental.pallas import tpu as pltpu
from jax.sharding import PartitionSpec as P

HEAD_DIM = 128
LANES = 128
norm_eps = 1e-05
DEAD = -1e30
HINT = 10**10


def swapped(array, axis, offset):
    size = lax.axis_size(axis)
    return lax.ppermute(array, axis, [(i, i ^ offset) for i in range(size)])


def stages(size, first):
    rounds, stride = [], first
    while stride < size:
        radix = 4 if size // stride % 4 == 0 else 2
        rounds.append([stride * k for k in range(1, radix)])
        stride *= radix
    return rounds


def tree_sum(terms):
    while len(terms) > 1:
        terms = [a + b for a, b in zip(terms[::2], terms[1::2])]
    return terms[0]


def vmem():
    return pl.BlockSpec(memory_space=pltpu.VMEM)


def in_hbm():
    return pl.BlockSpec(memory_space=pltpu.HBM)


def pinned(array):
    return pltpu.with_memory_space_constraint(array, pltpu.HBM)


def core_index():
    return lax.rem(lax.axis_index("seq"), 2)


def project_kernel(cuts, lengths_hbm, x_hbm, gain_hbm, wq_hbm, wk_hbm, wv_hbm, out_ref, rows_ref, lengths, x_ref, gain_ref, wq, wk, wv, acc, sems):
    pairs = [(x_hbm, x_ref), (gain_hbm, gain_ref), (wk_hbm, wk), (wv_hbm, wv)]
    for low, high in zip(cuts, cuts[1:]):
        part = pl.ds(low, high - low)
        pairs.append((wq_hbm.at[part], wq.at[part]))
    pairs.append((lengths_hbm, lengths))
    copies = [pltpu.make_async_copy(a, b, sems.at[n]) for n, (a, b) in enumerate(pairs)]
    for copy in copies:
        copy.start()
    copies[0].wait()
    copies[1].wait()
    x = x_ref[...].astype(jnp.float32)
    squares = jnp.sum(x * x, axis=1, keepdims=True)
    normed = (x * gain_ref[...]).astype(jnp.bfloat16)
    copies[2].wait()
    key = jnp.dot(normed, wk[...], preferred_element_type=jnp.float32)
    copies[3].wait()
    value = jnp.dot(normed, wv[...], preferred_element_type=jnp.float32)
    half = wq.shape[1] // 2
    heads = half // LANES
    squares = jnp.broadcast_to(squares, (x.shape[0], LANES))
    for g in range(2):
        out_ref[g, heads] = key[:, g * LANES : (g + 1) * LANES]
        out_ref[g, heads + 1] = value[:, g * LANES : (g + 1) * LANES]
        out_ref[g, heads + 2] = squares
    last = len(cuts) - 2
    for n, (low, high) in enumerate(zip(cuts, cuts[1:])):
        copies[4 + n].wait()
        part = jnp.dot(
            normed[:, low:high], wq[low:high, :], preferred_element_type=jnp.float32
        )
        if n == 0:
            acc[...] = part
        elif n < last:
            acc[...] += part
        else:
            query = acc[...] + part
    for g in range(2):
        for j in range(heads):
            at = g * half + j * LANES
            out_ref[g, j] = query[:, at : at + LANES]
    copies[-1].wait()
    for b in range(x.shape[0]):
        rows_ref[b : b + 1, :] = jnp.full((1, LANES), lengths[b], jnp.int32)


def project(lengths, x, gain, w_query, w_key, w_value):
    depth, width = w_query.shape
    batch = x.shape[0]
    step = min(depth // 2, 256)
    cuts = tuple(range(0, depth - step + 1, step)) + (depth - step // 2, depth)
    shape = (
        jax.ShapeDtypeStruct((2, width // 2 // LANES + 3, batch, LANES), jnp.float32),
        jax.ShapeDtypeStruct((batch, LANES), jnp.int32),
    )
    size = 2 * (w_query.size + w_key.size + w_value.size)
    return pl.pallas_call(
        lambda *refs: project_kernel(cuts, *refs),
        out_shape=shape,
        in_specs=[in_hbm()] * 6,
        out_specs=(vmem(), vmem()),
        scratch_shapes=[
            pltpu.SMEM(lengths.shape, lengths.dtype),
            pltpu.VMEM(x.shape, x.dtype),
            pltpu.VMEM((1, depth), gain.dtype),
            pltpu.VMEM(w_query.shape, w_query.dtype),
            pltpu.VMEM(w_key.shape, w_key.dtype),
            pltpu.VMEM(w_value.shape, w_value.dtype),
            pltpu.VMEM((batch, width), jnp.float32),
            pltpu.SemaphoreType.DMA((len(cuts) + 4,)),
        ],
        compiler_params=pltpu.CompilerParams(vmem_limit_bytes=size + (4 << 20)),
        cost_estimate=pl.CostEstimate(flops=batch * size, bytes_accessed=size, transcendentals=0),
        name="project",
    )(*(pinned(a) for a in (lengths, x, gain.reshape(1, depth), w_query, w_key, w_value)))


def attend_kernel(straight, width, rows_ref, q_ref, k_ref, v_ref, out_ref):
    batch, ctx = k_ref.shape[0], k_ref.shape[1]
    group = q_ref.shape[0] - 3
    me = lax.axis_index("seq")
    head = core_index() if straight else 1 - core_index()
    columns = pl.ds(pl.multiple_of(head * LANES, LANES), LANES)
    holds_new = me == 0
    row_scale = lax.rsqrt(q_ref[group + 2] / width + norm_eps)
    score_scale = 1.0 / math.sqrt(HEAD_DIM)
    lane = lax.broadcasted_iota(jnp.int32, (group, LANES), 1)
    sub = lax.broadcasted_iota(jnp.int32, (group, LANES), 0)
    position = me * ctx + lax.broadcasted_iota(jnp.int32, (1, ctx), 1)
    live = [position < rows_ref[b : b + 1, 0:1] for b in range(batch)]
    query, scores, own_score, new_value = [], [], [], []
    for b in range(batch):
        scale = row_scale[b : b + 1, :]
        query.append((q_ref[0:group, b, :] * scale).astype(jnp.bfloat16))
        new_key, value = (
            (q_ref[row, b : b + 1, :] * scale).astype(jnp.bfloat16).astype(jnp.float32)
            for row in (group, group + 1)
        )
        new_value.append(value)
        score = jnp.sum(query[b].astype(jnp.float32) * new_key, axis=1, keepdims=True)
        own_score.append(jnp.where(holds_new, score * score_scale, DEAD))
    for b in range(batch):
        score = lax.dot_general(
            query[b],
            k_ref[b, :, columns],
            (((1,), (1,)), ((), ())),
            preferred_element_type=jnp.float32,
        )
        scores.append(jnp.where(live[b], score * score_scale, DEAD))
    top = [
        jnp.maximum(jnp.max(scores[b], axis=1, keepdims=True), own_score[b]) for b in range(batch)
    ]
    weights = [jnp.where(live[b], jnp.exp(scores[b] - top[b]), 0.0) for b in range(batch)]
    own_weight = [jnp.where(holds_new, jnp.exp(own_score[b] - top[b]), 0.0) for b in range(batch)]
    total = [jnp.sum(weights[b], axis=1, keepdims=True) + own_weight[b] for b in range(batch)]
    tops = jnp.zeros((1, LANES), jnp.float32)
    sums = jnp.zeros((1, LANES), jnp.float32)
    for b in range(batch):
        high = weights[b].astype(jnp.bfloat16)
        low = (weights[b] - high.astype(jnp.float32)).astype(jnp.bfloat16)
        both = jnp.dot(
            jnp.concatenate([high, low], 0),
            v_ref[b, :, columns],
            preferred_element_type=jnp.float32,
        )
        out_ref[0:group, b, :] = both[:group] + both[group:] + own_weight[b] * new_value[b]
        spot = lane == sub + b * group
        tops = tops + jnp.sum(jnp.where(spot, top[b], 0.0), axis=0, keepdims=True)
        sums = sums + jnp.sum(jnp.where(spot, total[b], 0.0), axis=0, keepdims=True)
    blank = jnp.zeros((batch - 1, LANES), jnp.float32)
    out_ref[group] = jnp.concatenate([tops, blank], 0)
    out_ref[group + 1] = jnp.concatenate([sums, blank], 0)


def attend(straight, summed, key_cache, value_cache, lengths, width):
    batch = key_cache.shape[0]
    group = summed.shape[0] - 3
    size = key_cache.size + value_cache.size
    return pl.pallas_call(
        lambda *refs: attend_kernel(straight, width, *refs),
        out_shape=jax.ShapeDtypeStruct((group + 2, batch, LANES), jnp.float32),
        in_specs=[vmem()] * 4,
        out_specs=vmem(),
        compiler_params=pltpu.CompilerParams(vmem_limit_bytes=2 * size + (8 << 20)),
        cost_estimate=pl.CostEstimate(flops=HINT * 10, bytes_accessed=size, transcendentals=0),
        name="attend",
    )(lengths, summed, key_cache, value_cache)


def three_rows(row, count):
    rows, rest = [], row
    for _ in range(3):
        rows.append(rest.astype(jnp.bfloat16).astype(jnp.float32))
        rest = rest - rows[-1]
    rows.append(jnp.zeros((count - 3, row.shape[1]), jnp.float32))
    return jnp.concatenate(rows, 0)


def merge_kernel(last, count, *refs):
    parts, out_ref, wide = list(refs[:count]), refs[count], refs[-1]
    result = out_ref if last else wide.at[count]
    group, batch = parts[0].shape[0] - 2, parts[0].shape[1]
    for j, part in enumerate(parts):
        if part.dtype != jnp.float32:
            wide[j] = part[...].astype(jnp.float32)
            parts[j] = wide.at[j]
    lane = lax.broadcasted_iota(jnp.int32, (group, LANES), 1)
    sub = lax.broadcasted_iota(jnp.int32, (group, LANES), 0)

    def row_of(part, tile):
        value = part[tile]
        return (value[0:1] + value[1:2]) + value[2:3]

    tops = [row_of(part, group) for part in parts]
    sums = [row_of(part, group + 1) for part in parts]
    top = tops[0]
    for other in tops[1:]:
        top = jnp.maximum(top, other)
    factors = [jnp.exp(own - top) for own in tops]
    total = tree_sum([f * s for f, s in zip(factors, sums)])
    if last:
        factors = factors + [total]
    for b in range(batch):
        spot = lane == sub + b * group
        columns = [
            jnp.sum(jnp.where(spot, f, 0.0), axis=1, keepdims=True) for f in factors
        ]
        mixed = tree_sum([part[0:group, b, :] * c for part, c in zip(parts, columns)])
        if last:
            mixed = (mixed / columns[-1]).astype(jnp.bfloat16).astype(jnp.float32)
        result[0:group, b, :] = mixed
    if not last:
        for tile, row in ((group, top), (group + 1, total)):
            out_ref[tile] = three_rows(row, batch).astype(jnp.bfloat16)
        out_ref[0:group] = result[0:group].astype(jnp.bfloat16)


def merge(parts, last):
    rows, batch, lanes = parts[0].shape
    if last:
        shape = jax.ShapeDtypeStruct((rows - 2, batch, lanes), jnp.float32)
    else:
        shape = jax.ShapeDtypeStruct((rows, batch, lanes), jnp.bfloat16)
    return pl.pallas_call(
        lambda *refs: merge_kernel(last, len(parts), *refs),
        out_shape=shape,
        in_specs=[vmem()] * len(parts),
        out_specs=vmem(),
        scratch_shapes=[pltpu.VMEM((len(parts) + 1, rows, batch, lanes), jnp.float32)],
        compiler_params=pltpu.CompilerParams(vmem_limit_bytes=4 << 20),
        name="merge",
    )(*parts)


def output_kernel(straight, steps, attended_ref, w_ref, *refs):
    out_ref = refs[-1]
    heads = attended_ref.shape[0]
    half = w_ref.shape[0] // 2
    head = core_index() if straight else 1 - core_index()
    rows = half // steps
    attended = jnp.concatenate([attended_ref[j] for j in range(heads)], 1).astype(jnp.bfloat16)
    total = refs[0][...] if len(refs) > 1 else None
    for n in range(steps):
        at = pl.ds(pl.multiple_of(head * half + n * rows, rows), rows)
        part = jnp.dot(
            attended[:, n * rows : (n + 1) * rows], w_ref[at, :], preferred_element_type=jnp.float32
        )
        total = part if total is None else total + part
    out_ref[...] = total


def output(straight, attended, w_out, so_far=()):
    depth, width = w_out.shape
    batch = attended.shape[1]
    size = w_out.size
    return pl.pallas_call(
        lambda *refs: output_kernel(straight, max(1, depth // 1024), *refs),
        out_shape=jax.ShapeDtypeStruct((batch, width), jnp.float32),
        in_specs=[vmem()] * (2 + len(so_far)),
        out_specs=vmem(),
        compiler_params=pltpu.CompilerParams(vmem_limit_bytes=2 * size + (4 << 20)),
        cost_estimate=pl.CostEstimate(flops=batch * size, bytes_accessed=size, transcendentals=0),
        name="output",
    )(attended, w_out, *so_far)


def add_kernel(*refs):
    refs[-1][...] = tree_sum([ref[...] for ref in refs[:-1]])


def added(parts):
    return pl.pallas_call(
        add_kernel,
        out_shape=jax.ShapeDtypeStruct(parts[0].shape, parts[0].dtype),
        in_specs=[vmem()] * len(parts),
        out_specs=vmem(),
        compiler_params=pltpu.CompilerParams(vmem_limit_bytes=4 << 20),
        cost_estimate=pl.CostEstimate(flops=HINT // 3, bytes_accessed=1024, transcendentals=0),
        name="added",
    )(*parts)


def pair_kernel(mine_ref, theirs_ref, keep_ref, send_ref):
    first = core_index() == 0
    low, high = (mine_ref[g] + theirs_ref[g] for g in range(2))
    keep_ref[...] = jnp.where(first, high, low)
    send_ref[...] = jnp.where(first, low, high)


def paired(mine, theirs):
    shape = jax.ShapeDtypeStruct(mine.shape[1:], mine.dtype)
    return pl.pallas_call(
        pair_kernel,
        out_shape=(shape, shape),
        in_specs=[vmem()] * 2,
        out_specs=(vmem(), vmem()),
        compiler_params=pltpu.CompilerParams(vmem_limit_bytes=4 << 20),
        cost_estimate=pl.CostEstimate(flops=HINT // 3, bytes_accessed=1024, transcendentals=0),
        name="paired",
    )(mine, theirs)


def gathered(array, offsets):
    return [swapped(array, "seq", k ^ 1) for k in [0] + offsets]


def local(hidden_in, norm_gain, w_query, w_key, w_value, key_cache, value_cache, lengths, w_out):
    seq, kv = lax.axis_size("seq"), lax.axis_size("kv")
    rounds = stages(seq, 2)
    partial, length_rows = project(lengths, hidden_in, norm_gain, w_query, w_key, w_value)
    straight = False
    summed, send = paired(partial, swapped(partial, "seq", 1))
    for n, offsets in enumerate(rounds):
        if n == 0:
            summed = added([summed] + [swapped(send, "seq", k ^ 1) for k in offsets])
        else:
            summed = added(gathered(summed, offsets))
            straight = not straight
    other = swapped(summed, "seq", 1)
    width = hidden_in.shape[1] * seq
    send = attend(straight, summed, key_cache, value_cache, length_rows, width)
    straight = not straight
    keep = attend(straight, other, key_cache, value_cache, length_rows, width)
    merged = merge([keep, swapped(send, "seq", 1)], False)
    for n, offsets in enumerate(rounds):
        merged = merge(gathered(merged, offsets), n == len(rounds) - 1)
        straight = not straight
    other = swapped(merged, "seq", 1)
    mixed = output(straight, merged, w_out)
    mixed = output(not straight, other, w_out, (mixed,))
    for offsets in stages(kv, 1):
        mixed = tree_sum([mixed] + [swapped(mixed, "kv", k) for k in offsets])
    return (hidden_in.astype(jnp.float32) + mixed).astype(jnp.bfloat16)


def solution(mesh):
    placed = (
        P(None, "seq"),
        P("seq"),
        P("seq", "kv"),
        P("seq", "kv"),
        P("seq", "kv"),
        P(None, "seq", "kv"),
        P(None, "seq", "kv"),
        P(),
        P("kv", "seq"),
    )
    return jax.shard_map(
        local, mesh=mesh, in_specs=placed, out_specs=P(None, "seq"), check_vma=False
    )
```

```python
import math

import jax
import jax.numpy as jnp
from jax import lax
from jax.experimental import pallas as pl
from jax.experimental.pallas import tpu as pltpu
from jax.sharding import PartitionSpec as P

HEAD_DIM = 128
LANES = 128
norm_eps = 1e-05
DEAD = -1e30
HINT = 10**10


def swapped(array, axis, offset):
    size = lax.axis_size(axis)
    return lax.ppermute(array, axis, [(i, i ^ offset) for i in range(size)])


def stages(size, first):
    rounds, stride = [], first
    while stride < size:
        radix = 4 if size // stride % 4 == 0 else 2
        rounds.append([stride * k for k in range(1, radix)])
        stride *= radix
    return rounds


def tree_sum(terms):
    while len(terms) > 1:
        terms = [a + b for a, b in zip(terms[::2], terms[1::2])]
    return terms[0]


def vmem():
    return pl.BlockSpec(memory_space=pltpu.VMEM)


def in_hbm():
    return pl.BlockSpec(memory_space=pltpu.HBM)


def pinned(array):
    return pltpu.with_memory_space_constraint(array, pltpu.HBM)


def core_index():
    return lax.rem(lax.axis_index("seq"), 2)


def project_kernel(cuts, lengths_hbm, x_hbm, gain_hbm, wq_hbm, wk_hbm, wv_hbm, out_ref, rows_ref, lengths, x_ref, gain_ref, wq, wk, wv, acc, sems):
    pairs = [(x_hbm, x_ref), (gain_hbm, gain_ref), (wk_hbm, wk), (wv_hbm, wv)]
    for low, high in zip(cuts, cuts[1:]):
        part = pl.ds(low, high - low)
        pairs.append((wq_hbm.at[part], wq.at[part]))
    pairs.append((lengths_hbm, lengths))
    copies = [pltpu.make_async_copy(a, b, sems.at[n]) for n, (a, b) in enumerate(pairs)]
    for copy in copies:
        copy.start()
    copies[0].wait()
    copies[1].wait()
    x = x_ref[...].astype(jnp.float32)
    squares = jnp.sum(x * x, axis=1, keepdims=True)
    normed = (x * gain_ref[...]).astype(jnp.bfloat16)
    copies[2].wait()
    key = jnp.dot(normed, wk[...], preferred_element_type=jnp.float32)
    copies[3].wait()
    value = jnp.dot(normed, wv[...], preferred_element_type=jnp.float32)
    half = wq.shape[1] // 2
    heads = half // LANES
    squares = jnp.broadcast_to(squares, (x.shape[0], LANES))
    for g in range(2):
        out_ref[g, heads] = key[:, g * LANES : (g + 1) * LANES]
        out_ref[g, heads + 1] = value[:, g * LANES : (g + 1) * LANES]
        out_ref[g, heads + 2] = squares
    last = len(cuts) - 2
    for n, (low, high) in enumerate(zip(cuts, cuts[1:])):
        copies[4 + n].wait()
        part = jnp.dot(
            normed[:, low:high], wq[low:high, :], preferred_element_type=jnp.float32
        )
        if n == 0:
            acc[...] = part
        elif n < last:
            acc[...] += part
        else:
            query = acc[...] + part
    for g in range(2):
        for j in range(heads):
            at = g * half + j * LANES
            out_ref[g, j] = query[:, at : at + LANES]
    copies[-1].wait()
    for b in range(x.shape[0]):
        rows_ref[b : b + 1, :] = jnp.full((1, LANES), lengths[b], jnp.int32)


def project(lengths, x, gain, w_query, w_key, w_value):
    depth, width = w_query.shape
    batch = x.shape[0]
    step = min(depth // 2, 256)
    cuts = tuple(range(0, depth - step + 1, step)) + (depth - step // 2, depth)
    shape = (
        jax.ShapeDtypeStruct((2, width // 2 // LANES + 3, batch, LANES), jnp.float32),
        jax.ShapeDtypeStruct((batch, LANES), jnp.int32),
    )
    size = 2 * (w_query.size + w_key.size + w_value.size)
    return pl.pallas_call(
        lambda *refs: project_kernel(cuts, *refs),
        out_shape=shape,
        in_specs=[in_hbm()] * 6,
        out_specs=(vmem(), vmem()),
        scratch_shapes=[
            pltpu.SMEM(lengths.shape, lengths.dtype),
            pltpu.VMEM(x.shape, x.dtype),
            pltpu.VMEM((1, depth), gain.dtype),
            pltpu.VMEM(w_query.shape, w_query.dtype),
            pltpu.VMEM(w_key.shape, w_key.dtype),
            pltpu.VMEM(w_value.shape, w_value.dtype),
            pltpu.VMEM((batch, width), jnp.float32),
            pltpu.SemaphoreType.DMA((len(cuts) + 4,)),
        ],
        compiler_params=pltpu.CompilerParams(vmem_limit_bytes=size + (4 << 20)),
        cost_estimate=pl.CostEstimate(flops=batch * size, bytes_accessed=size, transcendentals=0),
        name="project",
    )(*(pinned(a) for a in (lengths, x, gain.reshape(1, depth), w_query, w_key, w_value)))


def attend_kernel(straight, width, rows_ref, q_ref, k_ref, v_ref, out_ref):
    batch, ctx = k_ref.shape[0], k_ref.shape[1]
    group = q_ref.shape[0] - 3
    me = lax.axis_index("seq")
    head = core_index() if straight else 1 - core_index()
    columns = pl.ds(pl.multiple_of(head * LANES, LANES), LANES)
    holds_new = me == 0
    row_scale = lax.rsqrt(q_ref[group + 2] / width + norm_eps)
    score_scale = 1.0 / math.sqrt(HEAD_DIM)
    lane = lax.broadcasted_iota(jnp.int32, (group, LANES), 1)
    sub = lax.broadcasted_iota(jnp.int32, (group, LANES), 0)
    position = me * ctx + lax.broadcasted_iota(jnp.int32, (1, ctx), 1)
    live = [position < rows_ref[b : b + 1, 0:1] for b in range(batch)]
    query, scores, own_score, new_value = [], [], [], []
    for b in range(batch):
        scale = row_scale[b : b + 1, :]
        query.append((q_ref[0:group, b, :] * scale).astype(jnp.bfloat16))
        new_key, value = (
            (q_ref[row, b : b + 1, :] * scale).astype(jnp.bfloat16).astype(jnp.float32)
            for row in (group, group + 1)
        )
        new_value.append(value)
        score = jnp.sum(query[b].astype(jnp.float32) * new_key, axis=1, keepdims=True)
        own_score.append(jnp.where(holds_new, score * score_scale, DEAD))
    for b in range(batch):
        score = lax.dot_general(
            query[b],
            k_ref[b, :, columns],
            (((1,), (1,)), ((), ())),
            preferred_element_type=jnp.float32,
        )
        scores.append(jnp.where(live[b], score * score_scale, DEAD))
    top = [
        jnp.maximum(jnp.max(scores[b], axis=1, keepdims=True), own_score[b]) for b in range(batch)
    ]
    weights = [jnp.where(live[b], jnp.exp(scores[b] - top[b]), 0.0) for b in range(batch)]
    own_weight = [jnp.where(holds_new, jnp.exp(own_score[b] - top[b]), 0.0) for b in range(batch)]
    total = [jnp.sum(weights[b], axis=1, keepdims=True) + own_weight[b] for b in range(batch)]
    tops = jnp.zeros((1, LANES), jnp.float32)
    sums = jnp.zeros((1, LANES), jnp.float32)
    for b in range(batch):
        high = weights[b].astype(jnp.bfloat16)
        low = (weights[b] - high.astype(jnp.float32)).astype(jnp.bfloat16)
        both = jnp.dot(
            jnp.concatenate([high, low], 0),
            v_ref[b, :, columns],
            preferred_element_type=jnp.float32,
        )
        out_ref[0:group, b, :] = both[:group] + both[group:] + own_weight[b] * new_value[b]
        spot = lane == sub + b * group
        tops = tops + jnp.sum(jnp.where(spot, top[b], 0.0), axis=0, keepdims=True)
        sums = sums + jnp.sum(jnp.where(spot, total[b], 0.0), axis=0, keepdims=True)
    blank = jnp.zeros((batch - 1, LANES), jnp.float32)
    out_ref[group] = jnp.concatenate([tops, blank], 0)
    out_ref[group + 1] = jnp.concatenate([sums, blank], 0)


def attend(straight, summed, key_cache, value_cache, lengths, width):
    batch = key_cache.shape[0]
    group = summed.shape[0] - 3
    size = key_cache.size + value_cache.size
    return pl.pallas_call(
        lambda *refs: attend_kernel(straight, width, *refs),
        out_shape=jax.ShapeDtypeStruct((group + 2, batch, LANES), jnp.float32),
        in_specs=[vmem()] * 4,
        out_specs=vmem(),
        compiler_params=pltpu.CompilerParams(vmem_limit_bytes=2 * size + (8 << 20)),
        cost_estimate=pl.CostEstimate(flops=HINT * 10, bytes_accessed=size, transcendentals=0),
        name="attend",
    )(lengths, summed, key_cache, value_cache)


def three_rows(row, count):
    rows, rest = [], row
    for _ in range(3):
        rows.append(rest.astype(jnp.bfloat16).astype(jnp.float32))
        rest = rest - rows[-1]
    rows.append(jnp.zeros((count - 3, row.shape[1]), jnp.float32))
    return jnp.concatenate(rows, 0)


def merge_kernel(last, count, *refs):
    parts, out_ref, wide = list(refs[:count]), refs[count], refs[-1]
    result = out_ref if last else wide.at[count]
    group, batch = parts[0].shape[0] - 2, parts[0].shape[1]
    for j, part in enumerate(parts):
        if part.dtype != jnp.float32:
            wide[j] = part[...].astype(jnp.float32)
            parts[j] = wide.at[j]
    lane = lax.broadcasted_iota(jnp.int32, (group, LANES), 1)
    sub = lax.broadcasted_iota(jnp.int32, (group, LANES), 0)

    def row_of(part, tile):
        value = part[tile]
        return (value[0:1] + value[1:2]) + value[2:3]

    tops = [row_of(part, group) for part in parts]
    sums = [row_of(part, group + 1) for part in parts]
    top = tops[0]
    for other in tops[1:]:
        top = jnp.maximum(top, other)
    factors = [jnp.exp(own - top) for own in tops]
    total = tree_sum([f * s for f, s in zip(factors, sums)])
    if last:
        factors = factors + [total]
    for b in range(batch):
        spot = lane == sub + b * group
        columns = [
            jnp.sum(jnp.where(spot, f, 0.0), axis=1, keepdims=True) for f in factors
        ]
        mixed = tree_sum([part[0:group, b, :] * c for part, c in zip(parts, columns)])
        if last:
            mixed = (mixed / columns[-1]).astype(jnp.bfloat16).astype(jnp.float32)
        result[0:group, b, :] = mixed
    if not last:
        for tile, row in ((group, top), (group + 1, total)):
            out_ref[tile] = three_rows(row, batch).astype(jnp.bfloat16)
        out_ref[0:group] = result[0:group].astype(jnp.bfloat16)


def merge(parts, last):
    rows, batch, lanes = parts[0].shape
    if last:
        shape = jax.ShapeDtypeStruct((rows - 2, batch, lanes), jnp.float32)
    else:
        shape = jax.ShapeDtypeStruct((rows, batch, lanes), jnp.bfloat16)
    return pl.pallas_call(
        lambda *refs: merge_kernel(last, len(parts), *refs),
        out_shape=shape,
        in_specs=[vmem()] * len(parts),
        out_specs=vmem(),
        scratch_shapes=[pltpu.VMEM((len(parts) + 1, rows, batch, lanes), jnp.float32)],
        compiler_params=pltpu.CompilerParams(vmem_limit_bytes=4 << 20),
        name="merge",
    )(*parts)


def output_kernel(straight, steps, attended_ref, w_ref, *refs):
    out_ref = refs[-1]
    heads = attended_ref.shape[0]
    half = w_ref.shape[0] // 2
    head = core_index() if straight else 1 - core_index()
    rows = half // steps
    attended = jnp.concatenate([attended_ref[j] for j in range(heads)], 1).astype(jnp.bfloat16)
    total = refs[0][...] if len(refs) > 1 else None
    for n in range(steps):
        at = pl.ds(pl.multiple_of(head * half + n * rows, rows), rows)
        part = jnp.dot(
            attended[:, n * rows : (n + 1) * rows], w_ref[at, :], preferred_element_type=jnp.float32
        )
        total = part if total is None else total + part
    out_ref[...] = total


def output(straight, attended, w_out, so_far=()):
    depth, width = w_out.shape
    batch = attended.shape[1]
    size = w_out.size
    return pl.pallas_call(
        lambda *refs: output_kernel(straight, max(1, depth // 1024), *refs),
        out_shape=jax.ShapeDtypeStruct((batch, width), jnp.float32),
        in_specs=[vmem()] * (2 + len(so_far)),
        out_specs=vmem(),
        compiler_params=pltpu.CompilerParams(vmem_limit_bytes=2 * size + (4 << 20)),
        cost_estimate=pl.CostEstimate(flops=batch * size, bytes_accessed=size, transcendentals=0),
        name="output",
    )(attended, w_out, *so_far)


def add_kernel(*refs):
    refs[-1][...] = tree_sum([ref[...] for ref in refs[:-1]])


def added(parts):
    return pl.pallas_call(
        add_kernel,
        out_shape=jax.ShapeDtypeStruct(parts[0].shape, parts[0].dtype),
        in_specs=[vmem()] * len(parts),
        out_specs=vmem(),
        compiler_params=pltpu.CompilerParams(vmem_limit_bytes=4 << 20),
        cost_estimate=pl.CostEstimate(flops=HINT // 3, bytes_accessed=1024, transcendentals=0),
        name="added",
    )(*parts)


def pair_kernel(mine_ref, theirs_ref, keep_ref, send_ref):
    first = core_index() == 0
    low, high = (mine_ref[g] + theirs_ref[g] for g in range(2))
    keep_ref[...] = jnp.where(first, high, low)
    send_ref[...] = jnp.where(first, low, high)


def paired(mine, theirs):
    shape = jax.ShapeDtypeStruct(mine.shape[1:], mine.dtype)
    return pl.pallas_call(
        pair_kernel,
        out_shape=(shape, shape),
        in_specs=[vmem()] * 2,
        out_specs=(vmem(), vmem()),
        compiler_params=pltpu.CompilerParams(vmem_limit_bytes=4 << 20),
        cost_estimate=pl.CostEstimate(flops=HINT // 3, bytes_accessed=1024, transcendentals=0),
        name="paired",
    )(mine, theirs)


def gathered(array, offsets):
    return [swapped(array, "seq", k ^ 1) for k in [0] + offsets]


def local(hidden_in, norm_gain, w_query, w_key, w_value, key_cache, value_cache, lengths, w_out):
    seq, kv = lax.axis_size("seq"), lax.axis_size("kv")
    rounds = stages(seq, 2)
    partial, length_rows = project(lengths, hidden_in, norm_gain, w_query, w_key, w_value)
    straight = False
    summed, send = paired(partial, swapped(partial, "seq", 1))
    for n, offsets in enumerate(rounds):
        if n == 0:
            summed = added([summed] + [swapped(send, "seq", k ^ 1) for k in offsets])
        else:
            summed = added(gathered(summed, offsets))
            straight = not straight
    other = swapped(summed, "seq", 1)
    width = hidden_in.shape[1] * seq
    send = attend(straight, summed, key_cache, value_cache, length_rows, width)
    straight = not straight
    keep = attend(straight, other, key_cache, value_cache, length_rows, width)
    merged = merge([keep, swapped(send, "seq", 1)], False)
    crossed = merge([send, swapped(keep, "seq", 1)], False)
    for n, offsets in enumerate(rounds):
        if n == 0:
            parts = [crossed] + [swapped(merged, "seq", k ^ 1) for k in offsets]
        else:
            parts = gathered(merged, offsets)
        merged = merge(parts, n == len(rounds) - 1)
        straight = not straight
    other = swapped(merged, "seq", 1)
    mixed = output(straight, merged, w_out)
    mixed = output(not straight, other, w_out, (mixed,))
    for offsets in stages(kv, 1):
        mixed = tree_sum([mixed] + [swapped(mixed, "kv", k) for k in offsets])
    return (hidden_in.astype(jnp.float32) + mixed).astype(jnp.bfloat16)


def solution(mesh):
    placed = (
        P(None, "seq"),
        P("seq"),
        P("seq", "kv"),
        P("seq", "kv"),
        P("seq", "kv"),
        P(None, "seq", "kv"),
        P(None, "seq", "kv"),
        P(),
        P("kv", "seq"),
    )
    return jax.shard_map(
        local, mesh=mesh, in_specs=placed, out_specs=P(None, "seq"), check_vma=False
    )
```

```python
import math

import jax
import jax.numpy as jnp
from jax import lax
from jax.experimental import pallas as pl
from jax.experimental.pallas import tpu as pltpu
from jax.sharding import PartitionSpec as P

HEAD_DIM = 128
LANES = 128
norm_eps = 1e-05
DEAD = -1e30
HINT = 10**10


def swapped(array, axis, offset):
    size = lax.axis_size(axis)
    return lax.ppermute(array, axis, [(i, i ^ offset) for i in range(size)])


def stages(size, first):
    rounds, stride = [], first
    while stride < size:
        radix = 4 if size // stride % 4 == 0 else 2
        rounds.append([stride * k for k in range(1, radix)])
        stride *= radix
    return rounds


def tree_sum(terms):
    while len(terms) > 1:
        terms = [a + b for a, b in zip(terms[::2], terms[1::2])]
    return terms[0]


def vmem():
    return pl.BlockSpec(memory_space=pltpu.VMEM)


def in_hbm():
    return pl.BlockSpec(memory_space=pltpu.HBM)


def pinned(array):
    return pltpu.with_memory_space_constraint(array, pltpu.HBM)


def core_index():
    return lax.rem(lax.axis_index("seq"), 2)


def project_kernel(cuts, lengths_hbm, x_hbm, gain_hbm, wq_hbm, wk_hbm, wv_hbm, out_ref, rows_ref, lengths, x_ref, gain_ref, wq, wk, wv, acc, sems):
    pairs = [(x_hbm, x_ref), (gain_hbm, gain_ref), (wk_hbm, wk), (wv_hbm, wv)]
    for low, high in zip(cuts, cuts[1:]):
        part = pl.ds(low, high - low)
        pairs.append((wq_hbm.at[part], wq.at[part]))
    pairs.append((lengths_hbm, lengths))
    copies = [pltpu.make_async_copy(a, b, sems.at[n]) for n, (a, b) in enumerate(pairs)]
    for copy in copies:
        copy.start()
    copies[0].wait()
    copies[1].wait()
    x = x_ref[...].astype(jnp.float32)
    squares = jnp.sum(x * x, axis=1, keepdims=True)
    normed = (x * gain_ref[...]).astype(jnp.bfloat16)
    copies[2].wait()
    key = jnp.dot(normed, wk[...], preferred_element_type=jnp.float32)
    copies[3].wait()
    value = jnp.dot(normed, wv[...], preferred_element_type=jnp.float32)
    half = wq.shape[1] // 2
    heads = half // LANES
    squares = jnp.broadcast_to(squares, (x.shape[0], LANES))
    for g in range(2):
        out_ref[g, heads] = key[:, g * LANES : (g + 1) * LANES]
        out_ref[g, heads + 1] = value[:, g * LANES : (g + 1) * LANES]
        out_ref[g, heads + 2] = squares
    last = len(cuts) - 2
    for n, (low, high) in enumerate(zip(cuts, cuts[1:])):
        copies[4 + n].wait()
        if n < last:
            part = jnp.dot(
                normed[:, low:high], wq[low:high, :], preferred_element_type=jnp.float32
            )
            acc[...] = part if n == 0 else acc[...] + part
            continue
        for j in range(0, 2 * heads, 2):
            at = slice(j * LANES, (j + 2) * LANES)
            part = jnp.dot(
                normed[:, low:high], wq[low:high, at], preferred_element_type=jnp.float32
            )
            part = acc[:, at] + part
            for k in range(2):
                g, h = divmod(j + k, heads)
                out_ref[g, h] = part[:, k * LANES : (k + 1) * LANES]
    copies[-1].wait()
    for b in range(x.shape[0]):
        rows_ref[b : b + 1, :] = jnp.full((1, LANES), lengths[b], jnp.int32)


def project(lengths, x, gain, w_query, w_key, w_value):
    depth, width = w_query.shape
    batch = x.shape[0]
    step = min(depth // 2, 256)
    cuts = tuple(range(0, depth - step + 1, step)) + (depth - step // 2, depth)
    shape = (
        jax.ShapeDtypeStruct((2, width // 2 // LANES + 3, batch, LANES), jnp.float32),
        jax.ShapeDtypeStruct((batch, LANES), jnp.int32),
    )
    size = 2 * (w_query.size + w_key.size + w_value.size)
    return pl.pallas_call(
        lambda *refs: project_kernel(cuts, *refs),
        out_shape=shape,
        in_specs=[in_hbm()] * 6,
        out_specs=(vmem(), vmem()),
        scratch_shapes=[
            pltpu.SMEM(lengths.shape, lengths.dtype),
            pltpu.VMEM(x.shape, x.dtype),
            pltpu.VMEM((1, depth), gain.dtype),
            pltpu.VMEM(w_query.shape, w_query.dtype),
            pltpu.VMEM(w_key.shape, w_key.dtype),
            pltpu.VMEM(w_value.shape, w_value.dtype),
            pltpu.VMEM((batch, width), jnp.float32),
            pltpu.SemaphoreType.DMA((len(cuts) + 4,)),
        ],
        compiler_params=pltpu.CompilerParams(vmem_limit_bytes=size + (4 << 20)),
        cost_estimate=pl.CostEstimate(flops=batch * size, bytes_accessed=size, transcendentals=0),
        name="project",
    )(*(pinned(a) for a in (lengths, x, gain.reshape(1, depth), w_query, w_key, w_value)))


def attend_kernel(straight, width, rows_ref, q_ref, k_ref, v_ref, out_ref):
    batch, ctx = k_ref.shape[0], k_ref.shape[1]
    group = q_ref.shape[0] - 3
    me = lax.axis_index("seq")
    head = core_index() if straight else 1 - core_index()
    columns = pl.ds(pl.multiple_of(head * LANES, LANES), LANES)
    holds_new = me == 0
    row_scale = lax.rsqrt(q_ref[group + 2] / width + norm_eps)
    score_scale = 1.0 / math.sqrt(HEAD_DIM)
    lane = lax.broadcasted_iota(jnp.int32, (group, LANES), 1)
    sub = lax.broadcasted_iota(jnp.int32, (group, LANES), 0)
    position = me * ctx + lax.broadcasted_iota(jnp.int32, (1, ctx), 1)
    live = [position < rows_ref[b : b + 1, 0:1] for b in range(batch)]
    query, scores, own_score, new_value = [], [], [], []
    for b in range(batch):
        scale = row_scale[b : b + 1, :]
        query.append((q_ref[0:group, b, :] * scale).astype(jnp.bfloat16))
        new_key, value = (
            (q_ref[row, b : b + 1, :] * scale).astype(jnp.bfloat16).astype(jnp.float32)
            for row in (group, group + 1)
        )
        new_value.append(value)
        score = jnp.sum(query[b].astype(jnp.float32) * new_key, axis=1, keepdims=True)
        own_score.append(jnp.where(holds_new, score * score_scale, DEAD))
    for b in range(batch):
        score = lax.dot_general(
            query[b],
            k_ref[b, :, columns],
            (((1,), (1,)), ((), ())),
            preferred_element_type=jnp.float32,
        )
        scores.append(jnp.where(live[b], score * score_scale, DEAD))
    top = [
        jnp.maximum(jnp.max(scores[b], axis=1, keepdims=True), own_score[b]) for b in range(batch)
    ]
    weights = [jnp.where(live[b], jnp.exp(scores[b] - top[b]), 0.0) for b in range(batch)]
    own_weight = [jnp.where(holds_new, jnp.exp(own_score[b] - top[b]), 0.0) for b in range(batch)]
    total = [jnp.sum(weights[b], axis=1, keepdims=True) + own_weight[b] for b in range(batch)]
    tops = jnp.zeros((1, LANES), jnp.float32)
    sums = jnp.zeros((1, LANES), jnp.float32)
    for b in range(batch):
        high = weights[b].astype(jnp.bfloat16)
        low = (weights[b] - high.astype(jnp.float32)).astype(jnp.bfloat16)
        both = jnp.dot(
            jnp.concatenate([high, low], 0),
            v_ref[b, :, columns],
            preferred_element_type=jnp.float32,
        )
        out_ref[0:group, b, :] = both[:group] + both[group:] + own_weight[b] * new_value[b]
        spot = lane == sub + b * group
        tops = tops + jnp.sum(jnp.where(spot, top[b], 0.0), axis=0, keepdims=True)
        sums = sums + jnp.sum(jnp.where(spot, total[b], 0.0), axis=0, keepdims=True)
    blank = jnp.zeros((batch - 1, LANES), jnp.float32)
    out_ref[group] = jnp.concatenate([tops, blank], 0)
    out_ref[group + 1] = jnp.concatenate([sums, blank], 0)


def attend(straight, summed, key_cache, value_cache, lengths, width):
    batch = key_cache.shape[0]
    group = summed.shape[0] - 3
    size = key_cache.size + value_cache.size
    return pl.pallas_call(
        lambda *refs: attend_kernel(straight, width, *refs),
        out_shape=jax.ShapeDtypeStruct((group + 2, batch, LANES), jnp.float32),
        in_specs=[vmem()] * 4,
        out_specs=vmem(),
        compiler_params=pltpu.CompilerParams(vmem_limit_bytes=2 * size + (8 << 20)),
        cost_estimate=pl.CostEstimate(flops=HINT * 10, bytes_accessed=size, transcendentals=0),
        name="attend",
    )(lengths, summed, key_cache, value_cache)


def three_rows(row, count):
    rows, rest = [], row
    for _ in range(3):
        rows.append(rest.astype(jnp.bfloat16).astype(jnp.float32))
        rest = rest - rows[-1]
    rows.append(jnp.zeros((count - 3, row.shape[1]), jnp.float32))
    return jnp.concatenate(rows, 0)


def merge_kernel(last, count, *refs):
    parts, out_ref, wide = list(refs[:count]), refs[count], refs[-1]
    result = out_ref if last else wide.at[count]
    group, batch = parts[0].shape[0] - 2, parts[0].shape[1]
    for j, part in enumerate(parts):
        if part.dtype != jnp.float32:
            wide[j] = part[...].astype(jnp.float32)
            parts[j] = wide.at[j]
    lane = lax.broadcasted_iota(jnp.int32, (group, LANES), 1)
    sub = lax.broadcasted_iota(jnp.int32, (group, LANES), 0)

    def row_of(part, tile):
        value = part[tile]
        return (value[0:1] + value[1:2]) + value[2:3]

    tops = [row_of(part, group) for part in parts]
    sums = [row_of(part, group + 1) for part in parts]
    top = tops[0]
    for other in tops[1:]:
        top = jnp.maximum(top, other)
    factors = [jnp.exp(own - top) for own in tops]
    total = tree_sum([f * s for f, s in zip(factors, sums)])
    if last:
        factors = factors + [total]
    for b in range(batch):
        spot = lane == sub + b * group
        columns = [
            jnp.sum(jnp.where(spot, f, 0.0), axis=1, keepdims=True) for f in factors
        ]
        mixed = tree_sum([part[0:group, b, :] * c for part, c in zip(parts, columns)])
        if last:
            mixed = (mixed / columns[-1]).astype(jnp.bfloat16).astype(jnp.float32)
        result[0:group, b, :] = mixed
    if not last:
        for tile, row in ((group, top), (group + 1, total)):
            out_ref[tile] = three_rows(row, batch).astype(jnp.bfloat16)
        out_ref[0:group] = result[0:group].astype(jnp.bfloat16)


def merge(parts, last):
    rows, batch, lanes = parts[0].shape
    if last:
        shape = jax.ShapeDtypeStruct((rows - 2, batch, lanes), jnp.float32)
    else:
        shape = jax.ShapeDtypeStruct((rows, batch, lanes), jnp.bfloat16)
    return pl.pallas_call(
        lambda *refs: merge_kernel(last, len(parts), *refs),
        out_shape=shape,
        in_specs=[vmem()] * len(parts),
        out_specs=vmem(),
        scratch_shapes=[pltpu.VMEM((len(parts) + 1, rows, batch, lanes), jnp.float32)],
        compiler_params=pltpu.CompilerParams(vmem_limit_bytes=4 << 20),
        name="merge",
    )(*parts)


def output_kernel(straight, steps, attended_ref, w_ref, *refs):
    out_ref = refs[-1]
    heads = attended_ref.shape[0]
    half = w_ref.shape[0] // 2
    head = core_index() if straight else 1 - core_index()
    rows = half // steps
    attended = jnp.concatenate([attended_ref[j] for j in range(heads)], 1).astype(jnp.bfloat16)
    total = refs[0][...] if len(refs) > 1 else None
    for n in range(steps):
        at = pl.ds(pl.multiple_of(head * half + n * rows, rows), rows)
        part = jnp.dot(
            attended[:, n * rows : (n + 1) * rows], w_ref[at, :], preferred_element_type=jnp.float32
        )
        total = part if total is None else total + part
    out_ref[...] = total


def output(straight, attended, w_out, so_far=()):
    depth, width = w_out.shape
    batch = attended.shape[1]
    size = w_out.size
    return pl.pallas_call(
        lambda *refs: output_kernel(straight, max(1, depth // 1024), *refs),
        out_shape=jax.ShapeDtypeStruct((batch, width), jnp.float32),
        in_specs=[vmem()] * (2 + len(so_far)),
        out_specs=vmem(),
        compiler_params=pltpu.CompilerParams(vmem_limit_bytes=2 * size + (4 << 20)),
        cost_estimate=pl.CostEstimate(flops=batch * size, bytes_accessed=size, transcendentals=0),
        name="output",
    )(attended, w_out, *so_far)


def add_kernel(*refs):
    refs[-1][...] = tree_sum([ref[...] for ref in refs[:-1]])


def added(parts):
    return pl.pallas_call(
        add_kernel,
        out_shape=jax.ShapeDtypeStruct(parts[0].shape, parts[0].dtype),
        in_specs=[vmem()] * len(parts),
        out_specs=vmem(),
        compiler_params=pltpu.CompilerParams(vmem_limit_bytes=4 << 20),
        cost_estimate=pl.CostEstimate(flops=HINT // 3, bytes_accessed=1024, transcendentals=0),
        name="added",
    )(*parts)


def pair_kernel(mine_ref, theirs_ref, keep_ref, send_ref):
    first = core_index() == 0
    low, high = (mine_ref[g] + theirs_ref[g] for g in range(2))
    keep_ref[...] = jnp.where(first, high, low)
    send_ref[...] = jnp.where(first, low, high)


def paired(mine, theirs):
    shape = jax.ShapeDtypeStruct(mine.shape[1:], mine.dtype)
    return pl.pallas_call(
        pair_kernel,
        out_shape=(shape, shape),
        in_specs=[vmem()] * 2,
        out_specs=(vmem(), vmem()),
        compiler_params=pltpu.CompilerParams(vmem_limit_bytes=4 << 20),
        cost_estimate=pl.CostEstimate(flops=HINT // 3, bytes_accessed=1024, transcendentals=0),
        name="paired",
    )(mine, theirs)


def gathered(array, offsets):
    return [swapped(array, "seq", k ^ 1) for k in [0] + offsets]


def local(hidden_in, norm_gain, w_query, w_key, w_value, key_cache, value_cache, lengths, w_out):
    seq, kv = lax.axis_size("seq"), lax.axis_size("kv")
    rounds = stages(seq, 2)
    partial, length_rows = project(lengths, hidden_in, norm_gain, w_query, w_key, w_value)
    straight = False
    summed, send = paired(partial, swapped(partial, "seq", 1))
    for n, offsets in enumerate(rounds):
        if n == 0:
            summed = added([summed] + [swapped(send, "seq", k ^ 1) for k in offsets])
        else:
            summed = added(gathered(summed, offsets))
            straight = not straight
    other = swapped(summed, "seq", 1)
    width = hidden_in.shape[1] * seq
    send = attend(straight, summed, key_cache, value_cache, length_rows, width)
    straight = not straight
    keep = attend(straight, other, key_cache, value_cache, length_rows, width)
    merged = merge([keep, swapped(send, "seq", 1)], False)
    crossed = merge([send, swapped(keep, "seq", 1)], False)
    for n, offsets in enumerate(rounds):
        if n == 0:
            parts = [crossed] + [swapped(merged, "seq", k ^ 1) for k in offsets]
        else:
            parts = gathered(merged, offsets)
        merged = merge(parts, n == len(rounds) - 1)
        straight = not straight
    other = swapped(merged, "seq", 1)
    mixed = output(straight, merged, w_out)
    mixed = output(not straight, other, w_out, (mixed,))
    for offsets in stages(kv, 1):
        mixed = tree_sum([mixed] + [swapped(mixed, "kv", k) for k in offsets])
    return (hidden_in.astype(jnp.float32) + mixed).astype(jnp.bfloat16)


def solution(mesh):
    placed = (
        P(None, "seq"),
        P("seq"),
        P("seq", "kv"),
        P("seq", "kv"),
        P("seq", "kv"),
        P(None, "seq", "kv"),
        P(None, "seq", "kv"),
        P(),
        P("kv", "seq"),
    )
    return jax.shard_map(
        local, mesh=mesh, in_specs=placed, out_specs=P(None, "seq"), check_vma=False
    )
```

```python
import math

import jax
import jax.numpy as jnp
from jax import lax
from jax.experimental import pallas as pl
from jax.experimental.pallas import tpu as pltpu
from jax.sharding import PartitionSpec as P

HEAD_DIM = 128
LANES = 128
norm_eps = 1e-05
DEAD = -1e30
HINT = 10**10


def swapped(array, axis, offset):
    size = lax.axis_size(axis)
    return lax.ppermute(array, axis, [(i, i ^ offset) for i in range(size)])


def stages(size, first):
    rounds, stride = [], first
    while stride < size:
        radix = 4 if size // stride % 4 == 0 else 2
        rounds.append([stride * k for k in range(1, radix)])
        stride *= radix
    return rounds


def tree_sum(terms):
    while len(terms) > 1:
        terms = [a + b for a, b in zip(terms[::2], terms[1::2])]
    return terms[0]


def vmem():
    return pl.BlockSpec(memory_space=pltpu.VMEM)


def in_hbm():
    return pl.BlockSpec(memory_space=pltpu.HBM)


def pinned(array):
    return pltpu.with_memory_space_constraint(array, pltpu.HBM)


def core_index():
    return lax.rem(lax.axis_index("seq"), 2)


def project_kernel(cuts, lengths_hbm, x_hbm, gain_hbm, wq_hbm, wk_hbm, wv_hbm, out_ref, rows_ref, lengths, x_ref, gain_ref, wq, wk, wv, acc, sems):
    pairs = [(x_hbm, x_ref), (gain_hbm, gain_ref), (wk_hbm, wk), (wv_hbm, wv)]
    for low, high in zip(cuts, cuts[1:]):
        part = pl.ds(low, high - low)
        pairs.append((wq_hbm.at[part], wq.at[part]))
    pairs.append((lengths_hbm, lengths))
    copies = [pltpu.make_async_copy(a, b, sems.at[n]) for n, (a, b) in enumerate(pairs)]
    for copy in copies:
        copy.start()
    copies[0].wait()
    copies[1].wait()
    x = x_ref[...].astype(jnp.float32)
    squares = jnp.sum(x * x, axis=1, keepdims=True)
    normed = (x * gain_ref[...]).astype(jnp.bfloat16)
    copies[2].wait()
    key = jnp.dot(normed, wk[...], preferred_element_type=jnp.float32)
    copies[3].wait()
    value = jnp.dot(normed, wv[...], preferred_element_type=jnp.float32)
    half = wq.shape[1] // 2
    heads = half // LANES
    squares = jnp.broadcast_to(squares, (x.shape[0], LANES))
    for g in range(2):
        out_ref[g, heads] = key[:, g * LANES : (g + 1) * LANES]
        out_ref[g, heads + 1] = value[:, g * LANES : (g + 1) * LANES]
        out_ref[g, heads + 2] = squares
    last = len(cuts) - 2
    for n, (low, high) in enumerate(zip(cuts, cuts[1:])):
        copies[4 + n].wait()
        part = jnp.dot(
            normed[:, low:high], wq[low:high, :], preferred_element_type=jnp.float32
        )
        if n == 0:
            acc[...] = part
        elif n < last:
            acc[...] += part
        else:
            query = acc[...] + part
    for g in range(2):
        for j in range(heads):
            at = g * half + j * LANES
            out_ref[g, j] = query[:, at : at + LANES]
    copies[-1].wait()
    for b in range(x.shape[0]):
        rows_ref[b : b + 1, :] = jnp.full((1, LANES), lengths[b], jnp.int32)


def project(lengths, x, gain, w_query, w_key, w_value):
    depth, width = w_query.shape
    batch = x.shape[0]
    step = min(depth // 2, 512)
    cuts = tuple(range(0, depth - step + 1, step)) + (depth - step // 2, depth)
    shape = (
        jax.ShapeDtypeStruct((2, width // 2 // LANES + 3, batch, LANES), jnp.float32),
        jax.ShapeDtypeStruct((batch, LANES), jnp.int32),
    )
    size = 2 * (w_query.size + w_key.size + w_value.size)
    return pl.pallas_call(
        lambda *refs: project_kernel(cuts, *refs),
        out_shape=shape,
        in_specs=[in_hbm()] * 6,
        out_specs=(vmem(), vmem()),
        scratch_shapes=[
            pltpu.SMEM(lengths.shape, lengths.dtype),
            pltpu.VMEM(x.shape, x.dtype),
            pltpu.VMEM((1, depth), gain.dtype),
            pltpu.VMEM(w_query.shape, w_query.dtype),
            pltpu.VMEM(w_key.shape, w_key.dtype),
            pltpu.VMEM(w_value.shape, w_value.dtype),
            pltpu.VMEM((batch, width), jnp.float32),
            pltpu.SemaphoreType.DMA((len(cuts) + 4,)),
        ],
        compiler_params=pltpu.CompilerParams(vmem_limit_bytes=size + (4 << 20)),
        cost_estimate=pl.CostEstimate(flops=batch * size, bytes_accessed=size, transcendentals=0),
        name="project",
    )(*(pinned(a) for a in (lengths, x, gain.reshape(1, depth), w_query, w_key, w_value)))


def attend_kernel(straight, width, rows_ref, q_ref, k_ref, v_ref, out_ref):
    batch, ctx = k_ref.shape[0], k_ref.shape[1]
    group = q_ref.shape[0] - 3
    me = lax.axis_index("seq")
    head = core_index() if straight else 1 - core_index()
    columns = pl.ds(pl.multiple_of(head * LANES, LANES), LANES)
    holds_new = me == 0
    row_scale = lax.rsqrt(q_ref[group + 2] / width + norm_eps)
    score_scale = 1.0 / math.sqrt(HEAD_DIM)
    lane = lax.broadcasted_iota(jnp.int32, (group, LANES), 1)
    sub = lax.broadcasted_iota(jnp.int32, (group, LANES), 0)
    position = me * ctx + lax.broadcasted_iota(jnp.int32, (1, ctx), 1)
    live = [position < rows_ref[b : b + 1, 0:1] for b in range(batch)]
    query, scores, own_score, new_value = [], [], [], []
    for b in range(batch):
        scale = row_scale[b : b + 1, :]
        query.append((q_ref[0:group, b, :] * scale).astype(jnp.bfloat16))
        new_key, value = (
            (q_ref[row, b : b + 1, :] * scale).astype(jnp.bfloat16).astype(jnp.float32)
            for row in (group, group + 1)
        )
        new_value.append(value)
        score = jnp.sum(query[b].astype(jnp.float32) * new_key, axis=1, keepdims=True)
        own_score.append(jnp.where(holds_new, score * score_scale, DEAD))
    for b in range(batch):
        score = lax.dot_general(
            query[b],
            k_ref[b, :, columns],
            (((1,), (1,)), ((), ())),
            preferred_element_type=jnp.float32,
        )
        scores.append(jnp.where(live[b], score * score_scale, DEAD))
    top = [
        jnp.maximum(jnp.max(scores[b], axis=1, keepdims=True), own_score[b]) for b in range(batch)
    ]
    weights = [jnp.where(live[b], jnp.exp(scores[b] - top[b]), 0.0) for b in range(batch)]
    own_weight = [jnp.where(holds_new, jnp.exp(own_score[b] - top[b]), 0.0) for b in range(batch)]
    total = [jnp.sum(weights[b], axis=1, keepdims=True) + own_weight[b] for b in range(batch)]
    tops = jnp.zeros((1, LANES), jnp.float32)
    sums = jnp.zeros((1, LANES), jnp.float32)
    for b in range(batch):
        high = weights[b].astype(jnp.bfloat16)
        low = (weights[b] - high.astype(jnp.float32)).astype(jnp.bfloat16)
        both = jnp.dot(
            jnp.concatenate([high, low], 0),
            v_ref[b, :, columns],
            preferred_element_type=jnp.float32,
        )
        out_ref[0:group, b, :] = both[:group] + both[group:] + own_weight[b] * new_value[b]
        spot = lane == sub + b * group
        tops = tops + jnp.sum(jnp.where(spot, top[b], 0.0), axis=0, keepdims=True)
        sums = sums + jnp.sum(jnp.where(spot, total[b], 0.0), axis=0, keepdims=True)
    blank = jnp.zeros((batch - 1, LANES), jnp.float32)
    out_ref[group] = jnp.concatenate([tops, blank], 0)
    out_ref[group + 1] = jnp.concatenate([sums, blank], 0)


def attend(straight, summed, key_cache, value_cache, lengths, width):
    batch = key_cache.shape[0]
    group = summed.shape[0] - 3
    size = key_cache.size + value_cache.size
    return pl.pallas_call(
        lambda *refs: attend_kernel(straight, width, *refs),
        out_shape=jax.ShapeDtypeStruct((group + 2, batch, LANES), jnp.float32),
        in_specs=[vmem()] * 4,
        out_specs=vmem(),
        compiler_params=pltpu.CompilerParams(vmem_limit_bytes=2 * size + (8 << 20)),
        cost_estimate=pl.CostEstimate(flops=HINT * 10, bytes_accessed=size, transcendentals=0),
        name="attend",
    )(lengths, summed, key_cache, value_cache)


def three_rows(row, count):
    rows, rest = [], row
    for _ in range(3):
        rows.append(rest.astype(jnp.bfloat16).astype(jnp.float32))
        rest = rest - rows[-1]
    rows.append(jnp.zeros((count - 3, row.shape[1]), jnp.float32))
    return jnp.concatenate(rows, 0)


def merge_kernel(last, count, *refs):
    parts, out_ref, wide = list(refs[:count]), refs[count], refs[-1]
    result = out_ref if last else wide.at[count]
    group, batch = parts[0].shape[0] - 2, parts[0].shape[1]
    for j, part in enumerate(parts):
        if part.dtype != jnp.float32:
            wide[j] = part[...].astype(jnp.float32)
            parts[j] = wide.at[j]
    lane = lax.broadcasted_iota(jnp.int32, (group, LANES), 1)
    sub = lax.broadcasted_iota(jnp.int32, (group, LANES), 0)

    def row_of(part, tile):
        value = part[tile]
        return (value[0:1] + value[1:2]) + value[2:3]

    tops = [row_of(part, group) for part in parts]
    sums = [row_of(part, group + 1) for part in parts]
    top = tops[0]
    for other in tops[1:]:
        top = jnp.maximum(top, other)
    factors = [jnp.exp(own - top) for own in tops]
    total = tree_sum([f * s for f, s in zip(factors, sums)])
    if last:
        factors = factors + [total]
    for b in range(batch):
        spot = lane == sub + b * group
        columns = [
            jnp.sum(jnp.where(spot, f, 0.0), axis=1, keepdims=True) for f in factors
        ]
        mixed = tree_sum([part[0:group, b, :] * c for part, c in zip(parts, columns)])
        if last:
            mixed = (mixed / columns[-1]).astype(jnp.bfloat16).astype(jnp.float32)
        result[0:group, b, :] = mixed
    if not last:
        for tile, row in ((group, top), (group + 1, total)):
            out_ref[tile] = three_rows(row, batch).astype(jnp.bfloat16)
        out_ref[0:group] = result[0:group].astype(jnp.bfloat16)


def merge(parts, last):
    rows, batch, lanes = parts[0].shape
    if last:
        shape = jax.ShapeDtypeStruct((rows - 2, batch, lanes), jnp.float32)
    else:
        shape = jax.ShapeDtypeStruct((rows, batch, lanes), jnp.bfloat16)
    return pl.pallas_call(
        lambda *refs: merge_kernel(last, len(parts), *refs),
        out_shape=shape,
        in_specs=[vmem()] * len(parts),
        out_specs=vmem(),
        scratch_shapes=[pltpu.VMEM((len(parts) + 1, rows, batch, lanes), jnp.float32)],
        compiler_params=pltpu.CompilerParams(vmem_limit_bytes=4 << 20),
        name="merge",
    )(*parts)


def output_kernel(straight, steps, attended_ref, w_ref, *refs):
    out_ref = refs[-1]
    heads = attended_ref.shape[0]
    half = w_ref.shape[0] // 2
    head = core_index() if straight else 1 - core_index()
    rows = half // steps
    attended = jnp.concatenate([attended_ref[j] for j in range(heads)], 1).astype(jnp.bfloat16)
    total = refs[0][...] if len(refs) > 1 else None
    for n in range(steps):
        at = pl.ds(pl.multiple_of(head * half + n * rows, rows), rows)
        part = jnp.dot(
            attended[:, n * rows : (n + 1) * rows], w_ref[at, :], preferred_element_type=jnp.float32
        )
        total = part if total is None else total + part
    out_ref[...] = total


def output(straight, attended, w_out, so_far=()):
    depth, width = w_out.shape
    batch = attended.shape[1]
    size = w_out.size
    return pl.pallas_call(
        lambda *refs: output_kernel(straight, max(1, depth // 1024), *refs),
        out_shape=jax.ShapeDtypeStruct((batch, width), jnp.float32),
        in_specs=[vmem()] * (2 + len(so_far)),
        out_specs=vmem(),
        compiler_params=pltpu.CompilerParams(vmem_limit_bytes=2 * size + (4 << 20)),
        cost_estimate=pl.CostEstimate(flops=batch * size, bytes_accessed=size, transcendentals=0),
        name="output",
    )(attended, w_out, *so_far)


def add_kernel(*refs):
    refs[-1][...] = tree_sum([ref[...] for ref in refs[:-1]])


def added(parts):
    return pl.pallas_call(
        add_kernel,
        out_shape=jax.ShapeDtypeStruct(parts[0].shape, parts[0].dtype),
        in_specs=[vmem()] * len(parts),
        out_specs=vmem(),
        compiler_params=pltpu.CompilerParams(vmem_limit_bytes=4 << 20),
        cost_estimate=pl.CostEstimate(flops=HINT // 3, bytes_accessed=1024, transcendentals=0),
        name="added",
    )(*parts)


def pair_kernel(mine_ref, theirs_ref, keep_ref, send_ref):
    first = core_index() == 0
    low, high = (mine_ref[g] + theirs_ref[g] for g in range(2))
    keep_ref[...] = jnp.where(first, high, low)
    send_ref[...] = jnp.where(first, low, high)


def paired(mine, theirs):
    shape = jax.ShapeDtypeStruct(mine.shape[1:], mine.dtype)
    return pl.pallas_call(
        pair_kernel,
        out_shape=(shape, shape),
        in_specs=[vmem()] * 2,
        out_specs=(vmem(), vmem()),
        compiler_params=pltpu.CompilerParams(vmem_limit_bytes=4 << 20),
        cost_estimate=pl.CostEstimate(flops=HINT // 3, bytes_accessed=1024, transcendentals=0),
        name="paired",
    )(mine, theirs)


def gathered(array, offsets):
    return [swapped(array, "seq", k ^ 1) for k in [0] + offsets]


def local(hidden_in, norm_gain, w_query, w_key, w_value, key_cache, value_cache, lengths, w_out):
    seq, kv = lax.axis_size("seq"), lax.axis_size("kv")
    rounds = stages(seq, 2)
    partial, length_rows = project(lengths, hidden_in, norm_gain, w_query, w_key, w_value)
    straight = False
    summed, send = paired(partial, swapped(partial, "seq", 1))
    for n, offsets in enumerate(rounds):
        if n == 0:
            summed = added([summed] + [swapped(send, "seq", k ^ 1) for k in offsets])
        else:
            summed = added(gathered(summed, offsets))
            straight = not straight
    other = swapped(summed, "seq", 1)
    width = hidden_in.shape[1] * seq
    send = attend(straight, summed, key_cache, value_cache, length_rows, width)
    straight = not straight
    keep = attend(straight, other, key_cache, value_cache, length_rows, width)
    merged = merge([keep, swapped(send, "seq", 1)], False)
    crossed = merge([send, swapped(keep, "seq", 1)], False)
    for n, offsets in enumerate(rounds):
        if n == 0:
            parts = [crossed] + [swapped(merged, "seq", k ^ 1) for k in offsets]
        else:
            parts = gathered(merged, offsets)
        merged = merge(parts, n == len(rounds) - 1)
        straight = not straight
    other = swapped(merged, "seq", 1)
    mixed = output(straight, merged, w_out)
    mixed = output(not straight, other, w_out, (mixed,))
    for offsets in stages(kv, 1):
        mixed = tree_sum([mixed] + [swapped(mixed, "kv", k) for k in offsets])
    return (hidden_in.astype(jnp.float32) + mixed).astype(jnp.bfloat16)


def solution(mesh):
    placed = (
        P(None, "seq"),
        P("seq"),
        P("seq", "kv"),
        P("seq", "kv"),
        P("seq", "kv"),
        P(None, "seq", "kv"),
        P(None, "seq", "kv"),
        P(),
        P("kv", "seq"),
    )
    return jax.shard_map(
        local, mesh=mesh, in_specs=placed, out_specs=P(None, "seq"), check_vma=False
    )
```
